512 devices in a mesh: worker: 16 (over x, y_hi, core), fsdp: 32 (over y_lo, z).
Axes of the slice: x: 4, y: 4 (y_hi: 2, y_lo: 2; y = y_hi * 2 + y_lo), z: 16, core: 2. Of those that a mesh axis runs over, the one named last changes fastest.
Arguments:
- inputs: bfloat16 [16, 2, 4096, 8192], P('worker', None, 'fsdp'), may hold values from -6 to 6
- targets: bfloat16 [16, 2, 4096, 512], P('worker', None, 'fsdp'), may hold values from -6 to 6
- base: float32 [8192, 512], P('fsdp', 'worker'), may hold values from -6 to 6
- adapter_a: float32 [16, 64, 8192], P('worker', None, 'fsdp'), may hold values from -6 to 6
- adapter_b: float32 [16, 512, 64], P('worker'), may hold values from -3 to 3
Outputs:
- new_base: float32 [8192, 512], P('fsdp', 'worker')
- final_a: float32 [16, 64, 8192], P('worker', None, 'fsdp')
- final_b: float32 [16, 512, 64], P('worker')
The draws below stay inside these ranges and needn't reach their ends.
All inputs are finite; a program needn't handle non-finite values.
Results may differ from the reference program's by a relative error of at most 0.0048.
Values may be sent and summed in bfloat16 or wider, within the bound.
No kernel may reach another device: no remote copies, remote signals or barrier semaphores. Data moves between devices by JAX's collectives and lax.ppermute only.
A program may use at most 64 MiB of HBM per device.

```python
import jax
import jax.numpy as jnp
from jax import lax

D = 8192
KW = 512
R = 64
STEPS = 2
TOKENS = 4096
WORKERS = 16


def spiked(array, rng, source, target, parts, factor):
    def block_of(axis_at):
        return (jnp.arange(array.shape[axis_at]) // (array.shape[axis_at] // parts)).reshape((-1,) + (1,) * (array.ndim - 1 - axis_at))

    near = jax.random.permutation(rng, parts)[block_of(target)]
    other_side = (block_of(target) + parts // 2) % parts
    return jnp.where((block_of(source) == near) | (block_of(source) == other_side), factor * array, array)


def block_scale(stream_key, extent, shards, smallest, largest):
    def one(axis_at, blocks):
        heights = jax.random.uniform(jax.random.fold_in(jax.random.fold_in(stream_key, 6), axis_at), (blocks,), jnp.float32, smallest / len(shards), largest / len(shards))
        return jnp.repeat(jnp.exp(heights), extent[axis_at] // blocks).reshape((-1,) + (1,) * (len(extent) - axis_at - 1))

    loudness = one(*shards[0])
    for cut in shards[1:]:
        loudness = loudness * one(*cut)
    return loudness


def noise(key, dims, deviation, most, split=(), kind=jnp.bfloat16):
    drawn = jax.random.normal(key, dims, jnp.float32) * deviation
    if len(split) > 0:
        drawn = block_scale(key, dims, split, -0.22, 0.18) * drawn
    return jnp.clip(drawn, min=-most, max=most).astype(kind)


def heavy_noise(key, extent, deviation, limit, pieces, heavy, dtype=jnp.bfloat16):
    entries = deviation * jax.random.normal(key, extent, jnp.float32)
    if pieces:
        entries = entries * block_scale(key, extent, pieces, -0.22, 0.18)
    return jnp.clip(spiked(entries, jax.random.fold_in(key, 3), *heavy), -limit, limit).astype(dtype)


def setup_inputs(seed: int = 0) -> dict:
    keys = jax.random.split(jax.random.key(seed), 6)
    return {
        "inputs": heavy_noise(keys[0], (WORKERS, STEPS, TOKENS, D), 1.0, 6.0, ((0, 16), (2, 32)), (2, 3, 32, 2.75)),
        "targets": noise(keys[1], (WORKERS, STEPS, TOKENS, KW), 1.0, 6.0, ((0, 16), (2, 32))),
        "base": noise(keys[2], (D, KW), 1.0, 6.0, ((0, 32), (1, 16)), jnp.float32),
        "adapter_a": noise(keys[3], (WORKERS, R, D), 1.0, 6.0, ((0, 16), (2, 32)), jnp.float32),
        "adapter_b": noise(keys[4], (WORKERS, KW, R), 0.5, 3.0, ((0, 16),), jnp.float32),
    }


branch_scale = 0.25
rate_down = 200.0
rate_up = 20.0


def reference(inputs, targets, base, adapter_a, adapter_b):
    high = lax.Precision.HIGHEST
    scale = D ** -0.5
    base_half = base.astype(jnp.bfloat16)

    def train_worker(total, pack):
        tokens, wanted, a_start, b_start = pack
        adapter, upper = a_start, b_start
        for step in range(STEPS):
            keys_base = jnp.dot(tokens[step], base_half, preferred_element_type=jnp.float32) * scale
            a_half = adapter.astype(jnp.bfloat16)
            low = jnp.dot(tokens[step], a_half.T, preferred_element_type=jnp.float32) * scale
            output = keys_base + branch_scale * jnp.dot(low, upper.T, precision=high)
            error = (output - wanted[step].astype(jnp.float32)) / TOKENS
            grad_b = branch_scale * jnp.dot(error.T, low, precision=high)
            back = (branch_scale * jnp.dot(error, upper, precision=high)).astype(jnp.bfloat16)
            grad_a = jnp.dot(back.T, tokens[step], preferred_element_type=jnp.float32) * scale
            adapter = adapter - rate_down * grad_a
            upper = upper - rate_up * grad_b
        change = branch_scale * (jnp.dot(adapter.T, upper.T, precision=high) - jnp.dot(a_start.T, b_start.T, precision=high))
        return total + change, (adapter, upper)

    total, finals = lax.scan(train_worker, jnp.zeros(base.shape, jnp.float32), (inputs, targets, adapter_a, adapter_b))
    new_base = base + total / WORKERS
    return new_base, finals[0], finals[1]
```

```python
import jax
import jax.numpy as jnp
from jax import lax
from jax.experimental import pallas as pl
from jax.experimental.pallas import tpu as pltpu
from jax.sharding import Mesh
from jax.sharding import PartitionSpec as P

W = ("x", "yh", "c")
F = ("yl", "z")
NZ = 16

branch_scale = 0.25
rate_down = 200.0
rate_up = 20.0

bf16 = jnp.bfloat16
f32 = jnp.float32
HIGH = lax.Precision.HIGHEST
VMEM = pltpu.CompilerParams(vmem_limit_bytes=60 * 1024 * 1024)


def dot(a, b, ca, cb, precision=None):
    return lax.dot_general(a, b, (((ca,), (cb,)), ((), ())), precision=precision, preferred_element_type=f32)


def split(value):
    hi = value.astype(bf16)
    return hi, (value - hi.astype(f32)).astype(bf16)


def vmem(n):
    return [pl.BlockSpec(memory_space=pltpu.VMEM)] * n


def hbm(n):
    return [pl.BlockSpec(memory_space=pl.ANY)] * n


def smem():
    return pl.BlockSpec(memory_space=pltpu.SMEM)


def keys_kernel(idx, x_ref, xr0, xr1, y_ref, a_ref, *rest):
    pieces = rest[:8]
    sent_ref, later_ref, xs, bs, xsem, bsem = rest[8:]
    half = xs.shape[-1]
    scale = (2 * half) ** (-0.5)
    px, pyh, pc, pyl = idx[0], idx[1], idx[2], idx[3]
    rows = xs.shape[2]
    copies = []
    for j in range(2):
        copies.append(pltpu.make_async_copy(x_ref.at[j, :, pl.ds(pyl * half, half)], xs.at[j, pyl], xsem.at[j]))
    for j, got in enumerate((xr0, xr1)):
        copies.append(pltpu.make_async_copy(got, xs.at[j, 1 - pyl], xsem.at[2 + j]))
    for k, piece in enumerate(pieces):
        dc, dx = divmod(k, 4)
        for dy in range(2):
            w = lax.rem(px + 4 - dx, 4) * 4 + lax.rem(pyh + dy, 2) * 2 + lax.rem(pc + dc, 2)
            copies.append(pltpu.make_async_copy(piece.at[dy], bs.at[w], bsem.at[k * 2 + dy]))
    for copy in copies:
        copy.start()
    for copy in copies:
        copy.wait()
    cols = bs.shape[0] * bs.shape[1]
    tokens = xs[...].reshape(4 * rows, half)

    low = jnp.zeros((a_ref.shape[1], 2 * rows), f32)
    for z in range(NZ):
        n = a_ref.shape[2]
        low = low + dot(a_ref[z], tokens[: 2 * rows, z * n : (z + 1) * n], 1, 1)
    hi, lo = split(low * scale)
    sent_ref[2 * rows :, : 2 * rows] = hi
    sent_ref[2 * rows :, 2 * rows :] = lo

    def some(n, carry):
        block = bs[pl.ds(n * 4, 4)].reshape(128, half)
        part = dot(tokens, block, 1, 1) * scale
        for q in range(4):
            mine = (q % 2) == pyl
            wanted = jnp.where(mine, y_ref[q // 2, :, pl.ds(n * 128, 128)].astype(f32), 0.0)
            value = part[q * rows : (q + 1) * rows] - wanted
            if q < 2:
                sent_ref[q * rows : (q + 1) * rows, pl.ds(n * 128, 128)] = value.astype(bf16)
            else:
                later_ref[(q - 2) * rows : (q - 1) * rows, pl.ds(n * 128, 128)] = value
        return carry

    lax.fori_loop(0, cols // 128, some, 0)


def joined(blocks):
    return jnp.concatenate(
        [jnp.concatenate([blocks[2 * g], blocks[2 * g + 1]], axis=1) for g in range(NZ // 2)], axis=0
    )


def gradients(pyl, low, keys, up, xo, xr, out, total_rows):
    rows = xo.shape[0]
    output = keys + branch_scale * dot(low, up, 0, 0, HIGH)
    error = output / total_rows
    up_grad = branch_scale * dot(low, error, 1, 0, HIGH)
    back = (branch_scale * dot(up, error, 1, 1, HIGH)).astype(bf16)
    first, second = back[:, :rows], back[:, rows:]
    own = jnp.where(pyl == 0, first, second)
    other = jnp.where(pyl == 0, second, first)
    hi, lo = split(up_grad)
    n = xo.shape[1] // NZ
    for z in range(NZ):
        at = slice(z * n, (z + 1) * n)
        out[z, :64] = (dot(own, xo[:, at], 1, 0) + dot(other, xr[:, at], 1, 0)).astype(bf16)
        g, h = z // 2, z % 2
        out[z, 64:72] = hi[8 * g : 8 * g + 8, 256 * h : 256 * h + 256]
        out[z, 72:80] = lo[8 * g : 8 * g + 8, 256 * h : 256 * h + 256]


def first_kernel(total_rows, idx, own, got, blocks, xo, xr, out):
    rows = 2 * xo.shape[1]
    keys = own[:rows].astype(f32) + got[:rows].astype(f32)
    a, b = own[rows:].astype(f32), got[rows:].astype(f32)
    low = (a[:, :rows] + a[:, rows:]) + (b[:, :rows] + b[:, rows:])
    gradients(idx[3], low, keys, joined(blocks[...]), xo[0], xr[...], out, total_rows)


def low_kernel(idx, whole, xo, xr, out):
    n = whole.shape[2]
    rows = xo.shape[1]
    scale = (2 * xo.shape[2]) ** (-0.5)
    own = jnp.zeros((64, rows), f32)
    other = jnp.zeros((64, rows), f32)
    for z in range(NZ):
        own = own + dot(whole[z, :64], xo[0, :, z * n : (z + 1) * n], 1, 1)
        other = other + dot(whole[z, :64], xr[:, z * n : (z + 1) * n], 1, 1)
    first = idx[3] == 0
    out[:, :rows] = jnp.where(first, own, other) * scale
    out[:, rows:] = jnp.where(first, other, own) * scale


def second_kernel(total_rows, idx, own, got, low_own, low_got, whole, xo, xr, out):
    blocks = whole[:, 64:72].astype(f32) + whole[:, 72:80].astype(f32)
    gradients(
        idx[3], low_own[...] + low_got[...], own[...] + got[...], joined(blocks), xo[0], xr[...], out, total_rows
    )


def summed(parts):
    down = jnp.zeros((64, 256), f32)
    up = jnp.zeros((8, 256), f32)
    for z in range(NZ):
        down = down + parts[z, :64].astype(f32)
        up = up + (parts[z, 64:72].astype(f32) + parts[z, 72:80].astype(f32))
    return down, up


def update_kernel(scale, idx, parts, a_ref, blocks, a_out, b_out, copies):
    down, up = summed(parts)
    a = a_ref[...] - (rate_down * scale) * down
    b = blocks[idx[4]] - rate_up * up
    a_out[...] = a
    a_half = a.astype(bf16)
    hi, lo = split(b)
    b_out[...] = hi.astype(f32) + lo.astype(f32)
    for z in range(NZ):
        copies[z, :64] = a_half
        copies[z, 64:72] = hi
        copies[z, 72:80] = lo


def last_update_kernel(scale, parts, a_ref, b_ref, a_out, copies):
    down, up = summed(parts)
    a_out[...] = a_ref[...] - (rate_down * scale) * down
    b = b_ref[...] - rate_up * up
    for z in range(NZ):
        copies[z] = b


def change_kernel(a_ref, blocks, a_start, blocks_start, out, b_out):
    up = joined(blocks[...])
    left = jnp.concatenate([up, -joined(blocks_start[...])], axis=0)
    right = jnp.concatenate([a_ref[...], a_start[...]], axis=0)
    out[...] = branch_scale * dot(left, right, 0, 0, HIGH)
    b_out[...] = up.T


def merge_kernel(parts, base, out):
    total = parts[0]
    for w in range(1, parts.shape[0]):
        total = total + parts[w]
    out[...] = base[...] + (total * (1.0 / parts.shape[0])).T


def call(kernel, shapes, specs, *args, scratch=()):
    return pl.pallas_call(
        kernel,
        out_shape=shapes,
        in_specs=specs,
        scratch_shapes=scratch,
        compiler_params=VMEM,
    )(*args)


def shaped(dims, kind):
    return jax.ShapeDtypeStruct(dims, kind)


def own_half_spec(step, rows, half):
    return pl.BlockSpec((1, rows, half), lambda idx: (step, 0, idx[3]))


def with_tokens(kernel, step, idx, shape, inputs, args):
    tokens, got = inputs
    rows, half = got.shape
    return pl.pallas_call(
        kernel,
        out_shape=shape,
        grid_spec=pltpu.PrefetchScalarGridSpec(
            num_scalar_prefetch=1,
            grid=(1,),
            in_specs=[pl.BlockSpec(a.shape, lambda i, s, n=a.ndim: (0,) * n) for a in args]
            + [
                pl.BlockSpec((1, rows, half), lambda i, s: (step, 0, s[3])),
                pl.BlockSpec((rows, half), lambda i, s: (0, 0)),
            ],
            out_specs=pl.BlockSpec(shape.shape, lambda i, s, n=len(shape.shape): (0,) * n),
        ),
        compiler_params=VMEM,
    )(idx, *args, tokens, got)


def swap(value, axis):
    return lax.ppermute(value, axis, [(0, 1), (1, 0)])


def shift(value, axis, by, count):
    return lax.ppermute(value, axis, [(i, (i + by) % count) for i in range(count)])


def gather_z(value):
    copies = jnp.broadcast_to(value, (NZ, *value.shape))
    return lax.all_to_all(copies, "z", 0, 0, tiled=True)


def exchange_z(parts):
    return lax.all_to_all(parts, "z", 0, 0, tiled=True)


def local(inputs, targets, base, adapter_a, adapter_b):
    tokens = inputs[0]
    a_start = adapter_a[0]
    steps, rows, width = tokens.shape
    half = width // 2
    scale = width ** (-0.5)
    total_rows = float(rows * 2 * NZ)
    idx = jnp.stack([lax.axis_index(n) for n in ("x", "yh", "c", "yl", "z")]).astype(jnp.int32)
    away = (1 - lax.axis_index("yl")) * half

    blocks = adapter_b[0].T.reshape(8, 8, 2, 256).transpose(0, 2, 1, 3).reshape(NZ, 8, 256)

    send0 = lax.dynamic_slice(tokens, (0, 0, away), (1, rows, half))[0]
    got0 = swap(send0, "yl")
    cols = gather_z(base.T.astype(bf16))
    cols = cols.transpose(1, 0, 2).reshape(cols.shape[1], half)
    pair = jnp.stack([cols, swap(cols, "yh")])
    near = [pair, shift(pair, "x", 1, 4), shift(pair, "x", 2, 4), shift(pair, "x", 3, 4)]
    send1 = lax.dynamic_slice(tokens, (1, 0, away), (1, rows, half))[0]
    got1 = swap(send1, "yl")
    a_whole = gather_z(a_start.astype(bf16))
    pieces = near + [swap(piece, "c") for piece in near]

    sent, later = pl.pallas_call(
        keys_kernel,
        out_shape=(shaped((2 * rows + 64, 512), bf16), shaped((2 * rows, 512), f32)),
        in_specs=[smem()] + hbm(3) + vmem(2) + hbm(8),
        scratch_shapes=[
            pltpu.VMEM((2, 2, rows, half), bf16),
            pltpu.VMEM((16, 32, half), bf16),
            pltpu.SemaphoreType.DMA((4,)),
            pltpu.SemaphoreType.DMA((16,)),
        ],
        compiler_params=VMEM,
    )(idx, tokens, got0, got1, targets[0], a_whole, *pieces)

    got_sent = swap(sent, "yl")
    got_later = swap(later, "yl")
    payload = shaped((NZ, 80, 256), bf16)

    def first(idx_ref, *refs):
        first_kernel(total_rows, idx_ref, *refs)

    parts = exchange_z(with_tokens(first, 0, idx, payload, (tokens, got0), (sent, got_sent, blocks)))

    def update(*refs):
        update_kernel(scale, *refs)

    a_next, b_next, copies = call(
        update,
        (shaped((64, 256), f32), shaped((8, 256), f32), payload),
        [smem()] + vmem(3),
        idx,
        parts,
        a_start,
        blocks,
    )
    whole = exchange_z(copies)
    low = with_tokens(low_kernel, 1, idx, shaped((64, 2 * rows), f32), (tokens, got1), (whole,))
    got_low = swap(low, "yl")

    def second(idx_ref, *refs):
        second_kernel(total_rows, idx_ref, *refs)

    parts = exchange_z(
        with_tokens(second, 1, idx, payload, (tokens, got1), (later, got_later, low, got_low, whole))
    )

    def last_update(*refs):
        last_update_kernel(scale, *refs)

    a_last, copies = call(
        last_update, (shaped((64, 256), f32), shaped((NZ, 8, 256), f32)), vmem(3), parts, a_next, b_next
    )
    blocks_last = exchange_z(copies)
    change, b_last = call(
        change_kernel,
        (shaped((512, 256), f32), shaped((512, 64), f32)),
        vmem(4),
        a_last,
        blocks_last,
        a_start,
        blocks,
    )
    merged = lax.all_to_all(change.reshape(16, 32, 256), W, 0, 0, tiled=True)
    new_base = call(merge_kernel, shaped(base.shape, f32), vmem(2), merged, base)
    return (new_base, a_last[None], b_last[None])


def solution(mesh):
    finer = Mesh(mesh.devices.reshape(4, 2, 2, 2, NZ), (*W, *F))
    return jax.shard_map(
        local,
        mesh=finer,
        in_specs=(
            P(W, None, F, None),
            P(W, None, F, None),
            P(F, W),
            P(W, None, F),
            P(W, None, None),
        ),
        out_specs=(P(F, W), P(W, None, F), P(W, None, None)),
        check_vma=False,
    )
```

```python
import jax
import jax.numpy as jnp
from jax import lax
from jax.experimental import pallas as pl
from jax.experimental.pallas import tpu as pltpu
from jax.sharding import Mesh
from jax.sharding import PartitionSpec as P

W = ("x", "yh", "c")
F = ("yl", "z")
NZ = 16

branch_scale = 0.25
rate_down = 200.0
rate_up = 20.0

bf16 = jnp.bfloat16
f32 = jnp.float32
HIGH = lax.Precision.HIGHEST
VMEM = pltpu.CompilerParams(vmem_limit_bytes=60 * 1024 * 1024)


def dot(a, b, ca, cb, precision=None):
    return lax.dot_general(a, b, (((ca,), (cb,)), ((), ())), precision=precision, preferred_element_type=f32)


def split(value):
    hi = value.astype(bf16)
    return hi, (value - hi.astype(f32)).astype(bf16)


def vmem(n):
    return [pl.BlockSpec(memory_space=pltpu.VMEM)] * n


def hbm(n):
    return [pl.BlockSpec(memory_space=pl.ANY)] * n


def smem():
    return pl.BlockSpec(memory_space=pltpu.SMEM)


def low_kernel(pyl, whole, xo, xr, out):
    n = whole.shape[2]
    rows = xo.shape[1]
    scale = (2 * xo.shape[2]) ** (-0.5)
    own = jnp.zeros((64, rows), f32)
    other = jnp.zeros((64, rows), f32)
    for z in range(NZ):
        own = own + dot(whole[z, :64], xo[0, :, z * n : (z + 1) * n], 1, 1)
        other = other + dot(whole[z, :64], xr[:, z * n : (z + 1) * n], 1, 1)
    first = pyl == 0
    out[:, :rows] = jnp.where(first, own, other) * scale
    out[:, rows:] = jnp.where(first, other, own) * scale


def keys_kernel(step, idx, x_ref, xr_ref, after, y_ref, *rest):
    pieces = rest[:8]
    out, xs, bs, xsem, bsem = rest[8:]
    half = xs.shape[-1]
    rows = xs.shape[1]
    scale = (2 * half) ** (-0.5)
    px, pyh, pc, pyl = idx[0], idx[1], idx[2], idx[3]
    copies = [
        pltpu.make_async_copy(x_ref.at[step, :, pl.ds(pyl * half, half)], xs.at[pyl], xsem.at[0]),
        pltpu.make_async_copy(xr_ref, xs.at[1 - pyl], xsem.at[1]),
    ]
    loads = []
    for k, piece in enumerate(pieces):
        dc, dx = divmod(k, 4)
        for dy in range(2):
            w = lax.rem(pyh + dy, 2) * 2 + lax.rem(pc + dc, 2)
            loads.append(pltpu.make_async_copy(piece.at[dy], bs.at[dx, w], bsem.at[k * 2 + dy]))
    for copy in copies + loads:
        copy.start()
    for copy in copies:
        copy.wait()
    tokens = xs[...].reshape(2 * rows, half)
    for dx in range(4):
        for k in (dx, dx + 4):
            for dy in range(2):
                loads[k * 2 + dy].wait()
        at = pl.ds(lax.rem(px + 4 - dx, 4) * 128, 128)
        part = dot(tokens, bs[dx].reshape(128, half), 1, 1) * scale
        wanted = y_ref[step, :, at].astype(f32)
        for q in range(2):
            rest_of = jnp.where(pyl == q, wanted, 0.0)
            out[q * rows : (q + 1) * rows, at] = (part[q * rows : (q + 1) * rows] - rest_of).astype(out.dtype)


def joined(blocks):
    return jnp.concatenate(
        [jnp.concatenate([blocks[2 * g], blocks[2 * g + 1]], axis=1) for g in range(NZ // 2)], axis=0
    )


def gradient_kernel(total_rows, pyl, own, got, low_own, low_got, blocks, xo, xr, out):
    if blocks.shape[1] == 8:
        up = joined(blocks[...])
    else:
        up = joined(blocks[:, 64:72].astype(f32) + blocks[:, 72:80].astype(f32))
    rows = xo.shape[1]
    low = low_own[...] + low_got[...]
    keys = own[...].astype(f32) + got[...].astype(f32)
    error = (keys + branch_scale * dot(low, up, 0, 0, HIGH)) / total_rows
    back = (branch_scale * dot(up, error, 1, 1, HIGH)).astype(bf16)
    hi, lo = split(branch_scale * dot(low, error, 1, 0, HIGH))
    first, second = back[:, :rows], back[:, rows:]
    own_back = jnp.where(pyl == 0, first, second)
    other_back = jnp.where(pyl == 0, second, first)
    n = xo.shape[2] // NZ
    for z in range(NZ):
        at = slice(z * n, (z + 1) * n)
        out[z, :64] = (dot(own_back, xo[0, :, at], 1, 0) + dot(other_back, xr[:, at], 1, 0)).astype(bf16)
        g, h = z // 2, z % 2
        out[z, 64:72] = hi[8 * g : 8 * g + 8, 256 * h : 256 * h + 256]
        out[z, 72:80] = lo[8 * g : 8 * g + 8, 256 * h : 256 * h + 256]


def summed(parts):
    down = parts[0, :64].astype(f32)
    up = parts[0, 64:72].astype(f32) + parts[0, 72:80].astype(f32)
    for z in range(1, NZ):
        down = down + parts[z, :64].astype(f32)
        up = up + (parts[z, 64:72].astype(f32) + parts[z, 72:80].astype(f32))
    return down, up


def update_kernel(scale, parts, a_ref, b_ref, a_out, b_out, copies):
    down, up = summed(parts)
    a = a_ref[...] - (rate_down * scale) * down
    b = b_ref[...] - rate_up * up
    a_out[...] = a
    a_half = a.astype(bf16)
    hi, lo = split(b)
    b_out[...] = hi.astype(f32) + lo.astype(f32)
    for z in range(NZ):
        copies[z, :64] = a_half
        copies[z, 64:72] = hi
        copies[z, 72:80] = lo


def last_update_kernel(scale, parts, a_ref, b_ref, a_out, copies):
    down, up = summed(parts)
    a_out[...] = a_ref[...] - (rate_down * scale) * down
    b = b_ref[...] - rate_up * up
    for z in range(NZ):
        copies[z] = b


def change_kernel(a_ref, blocks, a_start, blocks_start, out, b_out):
    up = joined(blocks[...])
    left = jnp.concatenate([up, -joined(blocks_start[...])], axis=0)
    right = jnp.concatenate([a_ref[...], a_start[...]], axis=0)
    out[...] = branch_scale * dot(left, right, 0, 0, HIGH)
    b_out[...] = up


def merge_kernel(parts, base, out):
    total = parts[0]
    for w in range(1, parts.shape[0]):
        total = total + parts[w]
    out[...] = base[...] + total * (1.0 / parts.shape[0])


def call(kernel, shapes, *args):
    return pl.pallas_call(
        kernel, out_shape=shapes, in_specs=vmem(len(args)), compiler_params=VMEM
    )(*args)


def shaped(dims, kind):
    return jax.ShapeDtypeStruct(dims, kind)


def with_tokens(kernel, step, idx, shape, tokens, got, args):
    rows, half = got.shape

    def body(s, *refs):
        kernel(s[3], *refs)

    return pl.pallas_call(
        body,
        out_shape=shape,
        grid_spec=pltpu.PrefetchScalarGridSpec(
            num_scalar_prefetch=1,
            grid=(1,),
            in_specs=[pl.BlockSpec(a.shape, lambda i, s, n=a.ndim: (0,) * n) for a in args]
            + [
                pl.BlockSpec((1, rows, half), lambda i, s: (step, 0, s[3])),
                pl.BlockSpec((rows, half), lambda i, s: (0, 0)),
            ],
            out_specs=pl.BlockSpec(shape.shape, lambda i, s, n=len(shape.shape): (0,) * n),
        ),
        compiler_params=VMEM,
    )(idx, *args, tokens, got)


def keys_of(step, idx, tokens, got, after, targets, pieces, kind):
    rows, half = got.shape

    def body(*refs):
        keys_kernel(step, *refs)

    return pl.pallas_call(
        body,
        out_shape=shaped((2 * rows, 512), kind),
        in_specs=[smem()] + hbm(3) + vmem(1) + hbm(8),
        scratch_shapes=[
            pltpu.VMEM((2, rows, half), bf16),
            pltpu.VMEM((4, 4, 32, half), bf16),
            pltpu.SemaphoreType.DMA((2,)),
            pltpu.SemaphoreType.DMA((16,)),
        ],
        compiler_params=VMEM,
    )(idx, tokens, got, after, targets, *pieces)


def swap(value, axis):
    return lax.ppermute(value, axis, [(0, 1), (1, 0)])


def shift(value, axis, by, count):
    return lax.ppermute(value, axis, [(i, (i + by) % count) for i in range(count)])


def exchange_z(parts):
    return lax.all_to_all(parts, "z", 0, 0, tiled=True)


def gather_z(value):
    return exchange_z(jnp.broadcast_to(value, (NZ, *value.shape)))


def whole_step(inputs, targets, base, adapter_a, adapter_b):
    tokens = inputs[0]
    a_start = adapter_a[0]
    _, rows, width = tokens.shape
    half = width // 2
    scale = width ** (-0.5)
    total_rows = float(rows * 2 * NZ)
    idx = jnp.stack([lax.axis_index(n) for n in ("x", "yh", "c", "yl", "z")]).astype(jnp.int32)
    away = (1 - lax.axis_index("yl")) * half
    blocks = adapter_b[0].T.reshape(8, 8, 2, 256).transpose(0, 2, 1, 3).reshape(NZ, 8, 256)
    block = lax.dynamic_index_in_dim(blocks, lax.axis_index("z"), 0, keepdims=False)

    def other_half(step):
        return lax.dynamic_slice(tokens, (step, 0, away), (1, rows, half))[0]

    send = lax.optimization_barrier(other_half(0))
    got0 = swap(send, "yl")
    cols = gather_z(base.T.astype(bf16))
    cols = cols.transpose(1, 0, 2).reshape(cols.shape[1], half)
    pair = jnp.stack([cols, swap(cols, "yh")])
    near = [pair] + [shift(pair, "x", d, 4) for d in (1, 2, 3)]
    a_whole = gather_z(a_start.astype(bf16))
    got1 = swap(other_half(1), "yl")
    pieces = near + [swap(piece, "c") for piece in near]

    low_shape = shaped((64, 2 * rows), f32)
    payload = shaped((NZ, 80, 256), bf16)

    def gradient(step, got, *args):
        return with_tokens(
            lambda *refs: gradient_kernel(total_rows, *refs), step, idx, payload, tokens, got, args
        )

    low = with_tokens(low_kernel, 0, idx, low_shape, tokens, got0, (a_whole,))
    got_low = swap(low, "yl")
    keys = keys_of(0, idx, tokens, got0, low, targets[0], pieces, bf16)
    got_keys = swap(keys, "yl")
    parts = exchange_z(gradient(0, got0, keys, got_keys, low, got_low, blocks))
    keys = keys_of(1, idx, tokens, got1, low, targets[0], pieces, f32)
    got_keys = swap(keys, "yl")

    a_next, block, copies = call(
        lambda *refs: update_kernel(scale, *refs),
        (shaped((64, 256), f32), shaped((8, 256), f32), payload),
        parts,
        a_start,
        block,
    )
    whole = exchange_z(copies)
    low = with_tokens(low_kernel, 1, idx, low_shape, tokens, got1, (whole,))
    got_low = swap(low, "yl")
    parts = exchange_z(gradient(1, got1, keys, got_keys, low, got_low, whole))
    a_last, copies = call(
        lambda *refs: last_update_kernel(scale, *refs),
        (shaped((64, 256), f32), shaped((NZ, 8, 256), f32)),
        parts,
        a_next,
        block,
    )
    blocks_last = exchange_z(copies)
    change, b_last = call(
        change_kernel, (shaped((512, 256), f32), shaped((64, 512), f32)), a_last, blocks_last, a_start, blocks
    )
    merged = lax.all_to_all(change.reshape(16, 32, 256), W, 0, 0, tiled=True)
    new_base = call(merge_kernel, shaped(base.shape[::-1], f32), merged, base.T)
    return (new_base.T, a_last[None], b_last.T[None])


def solution(mesh):
    finer = Mesh(mesh.devices.reshape(4, 2, 2, 2, NZ), (*W, *F))
    return jax.shard_map(
        whole_step,
        mesh=finer,
        in_specs=(
            P(W, None, F, None),
            P(W, None, F, None),
            P(F, W),
            P(W, None, F),
            P(W, None, None),
        ),
        out_specs=(P(F, W), P(W, None, F), P(W, None, None)),
        check_vma=False,
    )
```

```python
import jax
import jax.numpy as jnp
from jax import lax
from jax.experimental import pallas as pl
from jax.experimental.pallas import tpu as pltpu
from jax.sharding import Mesh
from jax.sharding import PartitionSpec as P

W = ("x", "yh", "c")
F = ("yl", "zh", "zl")
Q = ("yl", "zl")
NZ = 8


branch_scale = 0.25
rate_down = 200.0
rate_up = 20.0

bf16 = jnp.bfloat16
f32 = jnp.float32
HIGH = lax.Precision.HIGHEST
VMEM = pltpu.CompilerParams(vmem_limit_bytes=60 * 1024 * 1024)


def dot(a, b, ca, cb, precision=None):
    return lax.dot_general(a, b, (((ca,), (cb,)), ((), ())), precision=precision, preferred_element_type=f32)


def split(value):
    hi = value.astype(bf16)
    return hi, (value - hi.astype(f32)).astype(bf16)


def vmem(n):
    return [pl.BlockSpec(memory_space=pltpu.VMEM)] * n


def hbm(n):
    return [pl.BlockSpec(memory_space=pl.ANY)] * n


def smem():
    return pl.BlockSpec(memory_space=pltpu.SMEM)


def in_order(flag, first, second, axis):
    return jnp.concatenate([jnp.where(flag == 0, first, second), jnp.where(flag == 0, second, first)], axis=axis)


def pack_kernel(step, idx, x_ref, *rest):
    outs, sems = rest[:4], rest[4]
    yl, zl = idx[3], idx[5]
    n = 256
    copies = []
    for k, out in enumerate(outs):
        a, b = k % 2, k // 2
        start = lax.rem(yl + a, 2) * (2 * NZ * n) + lax.rem(zl + b, 2) * n
        for z in range(NZ):
            copies.append(
                pltpu.make_async_copy(
                    x_ref.at[step, :, pl.ds(pl.multiple_of(start + z * 2 * n, n), n)],
                    out.at[:, z * n : (z + 1) * n],
                    sems.at[k * NZ + z],
                )
            )
    for copy in copies:
        copy.start()
    for copy in copies:
        copy.wait()


def low_kernel(scale, idx, whole, own, gy, gz, gd, out):
    yl, zl = idx[3], idx[5]
    n = whole.shape[2]
    pairs = []
    for pair in ((own, gy), (gz, gd)):
        parts = []
        for piece in pair:
            part = dot(whole[0, :64], piece[:, :n], 1, 1)
            for z in range(1, NZ):
                part = part + dot(whole[z, :64], piece[:, z * n : (z + 1) * n], 1, 1)
            parts.append(part * scale)
        pairs.append(in_order(yl, *parts, axis=1))
    for y in range(2):
        out[2 * y + zl] = pairs[0]
        out[2 * y + 1 - zl] = pairs[1]


def keys_kernel(step, scale, idx, *rest):
    x_refs, y_ref, pieces = rest[:4], rest[5], rest[6:14]
    outs, (xs, bs, xsem, bsem) = rest[14:-4], rest[-4:]
    rows, quarter = xs.shape[2:]
    px, pyh, pc, yl, zl = idx[0], idx[1], idx[2], idx[3], idx[5]
    copies = []
    for k, ref in enumerate(x_refs):
        at = xs.at[lax.rem(zl + k // 2, 2), lax.rem(yl + k % 2, 2)]
        copies.append(pltpu.make_async_copy(ref, at, xsem.at[k]))
    loads = []
    for k, piece in enumerate(pieces):
        dc, dx = divmod(k, 4)
        for dy in range(2):
            w = lax.rem(pyh + dy, 2) * 2 + lax.rem(pc + dc, 2)
            loads.append(pltpu.make_async_copy(piece.at[dy], bs.at[dx, w], bsem.at[k * 2 + dy]))
    for copy in copies + loads:
        copy.start()
    for copy in copies:
        copy.wait()
    tokens = xs[...].reshape(4 * rows, quarter)
    for dx in range(4):
        for k in (dx, dx + 4):
            for dy in range(2):
                loads[k * 2 + dy].wait()
        at = pl.ds(pl.multiple_of(lax.rem(px + 4 - dx, 4) * 128, 128), 128)
        part = dot(tokens, bs[dx].reshape(128, quarter), 1, 1) * scale
        wanted = y_ref[step, :, at].astype(f32)
        less = [jnp.where(2 * zl + yl == q, wanted, 0.0) for q in range(4)]
        part = (part - jnp.concatenate(less, axis=0)).astype(bf16)
        pairs = part[: 2 * rows], part[2 * rows :]
        if len(outs) == 1:
            for y in range(2):
                for z in range(2):
                    outs[0][2 * y + z, :, at] = pairs[z]
        else:
            outs[0][:, at] = jnp.where(zl == 0, pairs[0], pairs[1])
            outs[1][:, at] = jnp.where(zl == 0, pairs[1], pairs[0])


def joined(blocks):
    return jnp.concatenate([jnp.concatenate([blocks[z, :8], blocks[z, 8:]], axis=1) for z in range(NZ)], axis=0)


def error_kernel(total_rows, low_parts, blocks, *rest):
    keys_parts, out = rest[:-1], rest[-1]
    if blocks.shape[1] == 16:
        up = joined(blocks[...])
    else:
        up = joined(blocks[:, 64:80].astype(f32) + blocks[:, 80:96].astype(f32))
    if len(keys_parts) == 1:
        keys_parts = [keys_parts[0].at[q] for q in range(4)]
    k = [part[...].astype(f32) for part in keys_parts]
    low = (low_parts[0] + low_parts[1]) + (low_parts[2] + low_parts[3])
    keys = (k[0] + k[1]) + (k[2] + k[3])
    error = (keys + branch_scale * dot(low, up, 0, 0, HIGH)) / total_rows
    tokens = error.shape[0]
    out[:, :tokens] = (branch_scale * dot(up, error, 1, 1, HIGH)).astype(bf16)
    out[:, tokens:] = (branch_scale * dot(low, error, 1, 0, HIGH)).astype(bf16)


def down_kernel(idx, mine, got, own, gy, gz, gd, out):
    yl = idx[3]
    rows = own.shape[0]
    backs = []
    for half in (mine, got):
        first, second = half[:, :rows], half[:, rows : 2 * rows]
        backs += [jnp.where(yl == 0, first, second), jnp.where(yl == 0, second, first)]
    up = (mine[:, 2 * rows :].astype(f32) + got[:, 2 * rows :].astype(f32)).astype(bf16)
    n = out.shape[2]
    for z in range(NZ):
        at = slice(z * n, (z + 1) * n)
        part = dot(backs[0], own[:, at], 1, 0) + dot(backs[1], gy[:, at], 1, 0)
        part = part + (dot(backs[2], gz[:, at], 1, 0) + dot(backs[3], gd[:, at], 1, 0))
        out[z, :64] = part.astype(bf16)
        out[z, 64:72] = up[8 * z : 8 * z + 8, :n]
        out[z, 72:80] = up[8 * z : 8 * z + 8, n:]


def summed(parts):
    result = parts[0].astype(f32)
    for k in range(1, parts.shape[0]):
        result = result + parts[k].astype(f32)
    return result


def update_kernel(scale, parts, a_ref, b_ref, a_out, b_out, copies):
    grads = summed(parts)
    a = a_ref[...] - (rate_down * scale) * grads[:64]
    hi, lo = split(b_ref[...] - rate_up * grads[64:])
    a_out[...] = a
    b_out[...] = hi.astype(f32) + lo.astype(f32)
    a_half = a.astype(bf16)
    for z in range(NZ):
        copies[z, :64] = a_half
        copies[z, 64:80] = hi
        copies[z, 80:96] = lo


def last_update_kernel(scale, parts, a_ref, b_ref, a_out, copies):
    grads = summed(parts)
    a_out[...] = a_ref[...] - (rate_down * scale) * grads[:64]
    b = b_ref[...] - rate_up * grads[64:]
    for z in range(NZ):
        copies[z] = b


def change_kernel(a_ref, blocks, a_start, blocks_start, out, b_out):
    up = joined(blocks[...])
    left = jnp.concatenate([up, -joined(blocks_start[...])], axis=0)
    right = jnp.concatenate([a_ref[...], a_start[...]], axis=0)
    out[...] = branch_scale * dot(left, right, 0, 0, HIGH)
    b_out[...] = up


def merge_kernel(parts, base, out):
    out[...] = base[...] + summed(parts) * (1.0 / parts.shape[0])


def shaped(dims, kind):
    return jax.ShapeDtypeStruct(dims, kind)


def call(kernel, shapes, *args):
    return pl.pallas_call(kernel, out_shape=shapes, in_specs=vmem(len(args)), compiler_params=VMEM)(*args)


def call_at(kernel, shapes, idx, *args):
    return pl.pallas_call(
        kernel, out_shape=shapes, in_specs=[smem()] + vmem(len(args)), compiler_params=VMEM
    )(idx, *args)


def pack(step, idx, tokens):
    def body(*refs):
        pack_kernel(step, *refs)

    rows, quarter = tokens.shape[1], tokens.shape[2] // 4
    return pl.pallas_call(
        body,
        out_shape=[shaped((rows, quarter), bf16)] * 4,
        in_specs=[smem()] + hbm(1),
        out_specs=hbm(4),
        scratch_shapes=[pltpu.SemaphoreType.DMA((4 * NZ,))],
        compiler_params=VMEM,
    )(idx, tokens)


def keys_of(step, scale, idx, xs, after, targets, pieces, shapes):
    rows, quarter = xs[0].shape

    def body(*refs):
        keys_kernel(step, scale, *refs)

    return pl.pallas_call(
        body,
        out_shape=shapes,
        in_specs=[smem()] + hbm(5) + vmem(1) + hbm(8),
        scratch_shapes=[
            pltpu.VMEM((2, 2, rows, quarter), bf16),
            pltpu.VMEM((4, 4, 32, quarter), bf16),
            pltpu.SemaphoreType.DMA((4,)),
            pltpu.SemaphoreType.DMA((16,)),
        ],
        compiler_params=VMEM,
    )(idx, *xs, after, targets, *pieces)


def swap(value, axis):
    return lax.ppermute(value, axis, [(0, 1), (1, 0)])


def swap_both(value):
    return lax.ppermute(value, Q, [(k, 3 - k) for k in range(4)])


def shift(value, axis, by, count):
    return lax.ppermute(value, axis, [(i, (i + by) % count) for i in range(count)])


def exchange(parts, axis):
    return lax.all_to_all(parts, axis, 0, 0, tiled=True)


def gather_z(value):
    return exchange(jnp.broadcast_to(value, (NZ, *value.shape)), "zh")


def whole_step(inputs, targets, base, adapter_a, adapter_b):
    tokens = inputs[0]
    a_start = adapter_a[0]
    _, rows, width = tokens.shape
    scale = width ** (-0.5)
    total_rows = float(rows * 4 * NZ)
    idx = jnp.stack([lax.axis_index(n) for n in (*W, *F[:1], "zh", "zl")]).astype(jnp.int32)
    blocks = adapter_b[0].T.reshape(NZ, 8, 2, 256).transpose(0, 2, 1, 3).reshape(NZ, 16, 256)
    block = lax.dynamic_index_in_dim(blocks, lax.axis_index("zh"), 0, keepdims=False)

    def quarters(step):
        own, to_y, to_z, to_both = pack(step, idx, tokens)
        return (own, swap(to_y, "yl"), swap(to_z, "zl"), swap_both(to_both))

    x0 = quarters(0)
    cols = gather_z(base.T.astype(bf16))
    cols = cols.transpose(1, 0, 2).reshape(cols.shape[1], width // 4)
    pair = jnp.stack([cols, swap(cols, "yh")])
    near = [pair] + [shift(pair, "x", d, 4) for d in (1, 2, 3)]
    whole = gather_z(a_start.astype(bf16))
    pieces = near + [swap(piece, "c") for piece in near]
    x1 = quarters(1)

    low_shape = shaped((4, 64, 2 * rows), f32)
    down_shape = shaped((NZ, 80, 256), bf16)

    def lows(whole, xs):
        part = call_at(lambda *refs: low_kernel(scale, *refs), low_shape, idx, whole, *xs)
        return exchange(part, Q)

    def gradients(xs, *args):
        mine = call(
            lambda *refs: error_kernel(total_rows, *refs), shaped((64, 2 * rows + 512), bf16), *args
        )
        got = swap(mine, "zl")
        return exchange(call_at(down_kernel, down_shape, idx, mine, got, *xs), "zh")

    low = lows(whole, x0)
    keys_shape = shaped((2 * rows, 512), bf16)
    keys = keys_of(0, scale, idx, x0, low, targets[0], pieces, shaped((4, *keys_shape.shape), bf16))
    keys = exchange(keys, Q)
    parts = gradients(x0, low, blocks, keys)

    own, other = keys_of(1, scale, idx, x1, low, targets[0], pieces, (keys_shape, keys_shape))
    keys = (own, swap(own, "yl"), swap(other, "zl"), swap_both(other))
    a_next, block, copies = call(
        lambda *refs: update_kernel(scale, *refs),
        (shaped((64, 256), f32), shaped((16, 256), f32), shaped((NZ, 96, 256), bf16)),
        parts,
        a_start,
        block,
    )
    whole = exchange(copies, "zh")
    low = lows(whole, x1)
    parts = gradients(x1, low, whole, *keys)
    a_last, copies = call(
        lambda *refs: last_update_kernel(scale, *refs),
        (shaped((64, 256), f32), shaped((NZ, 16, 256), f32)),
        parts,
        a_next,
        block,
    )
    blocks_last = exchange(copies, "zh")
    change, b_last = call(
        change_kernel, (shaped((512, 256), f32), shaped((64, 512), f32)), a_last, blocks_last, a_start, blocks
    )
    merged = exchange(change.reshape(16, 32, 256), W)
    new_base = call(merge_kernel, shaped(base.shape[::-1], f32), merged, base.T)
    return (new_base.T, a_last[None], b_last.T[None])


def solution(mesh):
    finer = Mesh(mesh.devices.reshape(4, 2, 2, 2, NZ, 2), (*W, *F))
    return jax.shard_map(
        whole_step,
        mesh=finer,
        in_specs=(
            P(W, None, F, None),
            P(W, None, F, None),
            P(F, W),
            P(W, None, F),
            P(W, None, None),
        ),
        out_specs=(P(F, W), P(W, None, F), P(W, None, None)),
        check_vma=False,
    )
```

```python
import jax
import jax.numpy as jnp
from jax import lax
from jax.experimental import pallas as pl
from jax.experimental.pallas import tpu as pltpu
from jax.sharding import Mesh
from jax.sharding import PartitionSpec as P

W = ("x", "yh", "c")
F = ("yl", "zh", "zl")
Q = ("yl", "zl")
NZ = 8


branch_scale = 0.25
rate_down = 200.0
rate_up = 20.0

bf16 = jnp.bfloat16
f32 = jnp.float32
HIGH = lax.Precision.HIGHEST
VMEM = pltpu.CompilerParams(vmem_limit_bytes=60 * 1024 * 1024)


def dot(a, b, ca, cb, precision=None):
    return lax.dot_general(a, b, (((ca,), (cb,)), ((), ())), precision=precision, preferred_element_type=f32)


def split(value):
    hi = value.astype(bf16)
    return hi, (value - hi.astype(f32)).astype(bf16)


def vmem(n):
    return [pl.BlockSpec(memory_space=pltpu.VMEM)] * n


def hbm(n):
    return [pl.BlockSpec(memory_space=pl.ANY)] * n


def smem():
    return pl.BlockSpec(memory_space=pltpu.SMEM)


def pack_kernel(idx, x_ref, *outs):
    yl, zl = idx[3], idx[5]
    n = 256
    for k, out in enumerate(outs):
        start = lax.rem(yl + k % 2, 2) * (2 * NZ * n) + lax.rem(zl + k // 2, 2) * n
        for z in range(NZ):
            out[0, :, z * n : (z + 1) * n] = x_ref[0, :, pl.ds(pl.multiple_of(start + z * 2 * n, n), n)]


def wide(value):
    return jnp.concatenate([value[16 * k : 16 * k + 16] for k in range(4)], axis=1)


def tall(value):
    n = value.shape[1] // 4
    return jnp.concatenate([value[:, k * n : k * n + n] for k in range(4)], axis=0)


def group_at(idx, k):
    return 2 * lax.rem(idx[3] + k % 2, 2) + lax.rem(idx[5] + k // 2, 2)


def partial_low(whole, tokens):
    n = whole.shape[2]
    part = dot(whole[0, :64], tokens[:, :n], 1, 1)
    for z in range(1, NZ):
        part = part + dot(whole[z, :64], tokens[:, z * n : (z + 1) * n], 1, 1)
    return part


def keys_kernel(step, scale, idx, *rest):
    x_refs, a_ref, y_ref, pieces = rest[:4], rest[4], rest[5], rest[6:14]
    outs, (xs, bs, xsem, bsem) = rest[14:-4], rest[-4:]
    rows, quarter = xs.shape[1:]
    px, pyh, pc = idx[0], idx[1], idx[2]
    places = [group_at(idx, k) for k in range(4)]
    copies = [pltpu.make_async_copy(ref.at[step], xs.at[k], xsem.at[k]) for k, ref in enumerate(x_refs)]
    loads = []
    for k, piece in enumerate(pieces):
        dc, dx = divmod(k, 4)
        for dy in range(2):
            w = lax.rem(pyh + dy, 2) * 2 + lax.rem(pc + dc, 2)
            loads.append(pltpu.make_async_copy(piece.at[dy], bs.at[dx, w], bsem.at[k * 2 + dy]))
    for copy in copies + loads:
        copy.start()
    for copy in copies:
        copy.wait()
    if step == 0:
        for k in range(4):
            hi, lo = split(partial_low(a_ref, xs[k]) * scale)
            outs[0][places[k], rows : rows + 16] = wide(hi)
            outs[0][places[k], rows + 16 :] = wide(lo)
    tokens = xs[...].reshape(4 * rows, quarter)
    for dx in range(4):
        for k in (dx, dx + 4):
            for dy in range(2):
                loads[k * 2 + dy].wait()
        at = pl.ds(pl.multiple_of(lax.rem(px + 4 - dx, 4) * 128, 128), 128)
        part = dot(tokens, bs[dx].reshape(128, quarter), 1, 1) * scale
        for k in range(4):
            value = part[k * rows : (k + 1) * rows]
            if k == 0:
                value = value - y_ref[step, :, at].astype(f32)
            if step == 0:
                outs[0][places[k], :rows, at] = value.astype(bf16)
            else:
                outs[k][:, at] = value.astype(bf16)


def low_kernel(scale, idx, whole, *rest):
    x_refs, out = rest[:4], rest[4]
    for k in range(4):
        at = group_at(idx, k)
        hi, lo = split(partial_low(whole, x_refs[k][0]) * scale)
        out[at, :64, :128] = hi
        out[at, :64, 128:] = lo
        out[at, 64:] = jnp.concatenate([whole[z, 64:] for z in range(NZ)], axis=0)


def quarter_of(blocks):
    value = blocks[:, :128].astype(f32) + blocks[:, 128:].astype(f32)
    halves = [
        jnp.concatenate([value[8 * (4 * r + c) : 8 * (4 * r + c) + 8] for c in range(4)], axis=1) for r in range(2)
    ]
    return jnp.concatenate(halves, axis=0)


def error_of(total_rows, keys, low, up, out):
    error = (keys + branch_scale * dot(low, up, 0, 0, HIGH)) / total_rows
    back = wide((branch_scale * dot(up, error, 1, 1, HIGH)).astype(bf16))
    hi, lo = split(branch_scale * dot(low, error, 1, 0, HIGH))
    for q in range(4):
        out[q, :16] = back
        out[q, 16:32] = hi[16 * q : 16 * q + 16]
        out[q, 32:] = lo[16 * q : 16 * q + 16]


def first_error_kernel(total_rows, parts, up_ref, out):
    rows = parts.shape[1] - 32
    k = [parts[q, :rows].astype(f32) for q in range(4)]
    low = [tall(parts[q, rows : rows + 16]).astype(f32) + tall(parts[q, rows + 16 :]).astype(f32) for q in range(4)]
    error_of(total_rows, (k[0] + k[1]) + (k[2] + k[3]), (low[0] + low[1]) + (low[2] + low[3]), up_ref[...], out)


def second_error_kernel(total_rows, parts, own, by_y, by_z, by_both, out):
    keys = (own[...].astype(f32) + by_y[...].astype(f32)) + (by_z[...].astype(f32) + by_both[...].astype(f32))
    low = [parts[q, :64, :128].astype(f32) + parts[q, :64, 128:].astype(f32) for q in range(4)]
    up = jnp.concatenate([quarter_of(parts[q, 64:]) for q in range(4)], axis=0)
    error_of(total_rows, keys, (low[0] + low[1]) + (low[2] + low[3]), up, out)


def down_kernel(idx, parts, *rest):
    x_refs, out = rest[:4], rest[4]
    backs = [tall(parts[group_at(idx, k), :16]) for k in range(4)]
    grads = [parts[q, 16:32].astype(f32) + parts[q, 32:].astype(f32) for q in range(4)]
    hi, lo = split((grads[0] + grads[1]) + (grads[2] + grads[3]))
    n = out.shape[2]
    for z in range(NZ):
        at = slice(z * n, (z + 1) * n)
        part = [dot(backs[k], x_refs[k][0, :, at], 1, 0) for k in range(4)]
        out[z, :64] = ((part[0] + part[1]) + (part[2] + part[3])).astype(bf16)
        r, c = z // 4, z % 4
        out[z, 64:, :128] = hi[8 * r : 8 * r + 8, 128 * c : 128 * c + 128]
        out[z, 64:, 128:] = lo[8 * r : 8 * r + 8, 128 * c : 128 * c + 128]


def summed(parts):
    result = parts[0].astype(f32)
    for k in range(1, parts.shape[0]):
        result = result + parts[k].astype(f32)
    return result


def update_kernel(scale, parts, a_ref, b_ref, a_out, b_out, copies):
    grads = summed(parts)
    a = a_ref[...] - (rate_down * scale) * grads[:64]
    hi, lo = split(b_ref[...] - rate_up * (grads[64:, :128] + grads[64:, 128:]))
    a_out[...] = a
    b_out[...] = hi.astype(f32) + lo.astype(f32)
    a_half = a.astype(bf16)
    for z in range(NZ):
        copies[z, :64] = a_half
        copies[z, 64:, :128] = hi
        copies[z, 64:, 128:] = lo


def last_update_kernel(scale, parts, a_ref, b_ref, a_out, copies):
    grads = summed(parts)
    a_out[...] = a_ref[...] - (rate_down * scale) * grads[:64]
    b = b_ref[...] - rate_up * (grads[64:, :128] + grads[64:, 128:])
    for k in range(4 * NZ):
        copies[k] = b


def change_kernel(a_ref, blocks, a_start, up_start, out, b_out):
    rows = []
    for q in range(4):
        yl, zl = q // 2, q % 2
        for r in range(2):
            at = [yl * 2 * NZ + (4 * r + c) * 2 + zl for c in range(4)]
            rows.append(jnp.concatenate([blocks[k] for k in at], axis=1))
    up = jnp.concatenate(rows, axis=0)
    left = jnp.concatenate([up, -up_start[...]], axis=0)
    right = jnp.concatenate([a_ref[...], a_start[...]], axis=0)
    out[...] = branch_scale * dot(left, right, 0, 0, HIGH)
    b_out[...] = up


def merge_kernel(parts, base, out):
    out[...] = base[...] + summed(parts) * (1.0 / parts.shape[0])


def shaped(dims, kind):
    return jax.ShapeDtypeStruct(dims, kind)


def call(kernel, shapes, *args):
    return pl.pallas_call(kernel, out_shape=shapes, in_specs=vmem(len(args)), compiler_params=VMEM)(*args)


def pack(idx, tokens):
    steps, rows, width = tokens.shape
    quarter = width // 4
    return pl.pallas_call(
        pack_kernel,
        out_shape=[shaped((steps, rows, quarter), bf16)] * 4,
        grid_spec=pltpu.PrefetchScalarGridSpec(
            num_scalar_prefetch=1,
            grid=(steps,),
            in_specs=[pl.BlockSpec((1, rows, width), lambda i, s: (i, 0, 0))],
            out_specs=[pl.BlockSpec((1, rows, quarter), lambda i, s: (i, 0, 0))] * 4,
        ),
        compiler_params=VMEM,
    )(idx, tokens)


def with_tokens(kernel, step, shape, idx, args, xs):
    _, rows, quarter = xs[0].shape
    return pl.pallas_call(
        kernel,
        out_shape=shape,
        grid_spec=pltpu.PrefetchScalarGridSpec(
            num_scalar_prefetch=1,
            grid=(1,),
            in_specs=[pl.BlockSpec(a.shape, lambda i, s, n=a.ndim: (0,) * n) for a in args]
            + [pl.BlockSpec((1, rows, quarter), lambda i, s: (step, 0, 0))] * 4,
            out_specs=pl.BlockSpec(shape.shape, lambda i, s, n=len(shape.shape): (0,) * n),
        ),
        compiler_params=VMEM,
    )(idx, *args, *xs)


def keys_of(step, scale, idx, xs, whole, targets, pieces, shapes):
    _, rows, quarter = xs[0].shape

    def body(*refs):
        keys_kernel(step, scale, *refs)

    return pl.pallas_call(
        body,
        out_shape=shapes,
        in_specs=[smem()] + hbm(4) + vmem(2) + hbm(8),
        scratch_shapes=[
            pltpu.VMEM((4, rows, quarter), bf16),
            pltpu.VMEM((4, 4, 32, quarter), bf16),
            pltpu.SemaphoreType.DMA((4,)),
            pltpu.SemaphoreType.DMA((16,)),
        ],
        compiler_params=VMEM,
    )(idx, *xs, whole, targets, *pieces)


def swap(value, axis):
    return lax.ppermute(value, axis, [(0, 1), (1, 0)])


def swap_both(value):
    return lax.ppermute(value, Q, [(k, 3 - k) for k in range(4)])


def shift(value, axis, by, count):
    return lax.ppermute(value, axis, [(i, (i + by) % count) for i in range(count)])


def exchange(parts, axis):
    return lax.all_to_all(parts, axis, 0, 0, tiled=True)


def gather_z(value):
    return exchange(jnp.broadcast_to(value, (NZ, *value.shape)), "zh")


def whole_step(inputs, targets, base, adapter_a, adapter_b):
    tokens = inputs[0]
    a_start = adapter_a[0]
    _, rows, width = tokens.shape
    scale = width ** (-0.5)
    total_rows = float(rows * 4 * NZ)
    idx = jnp.stack([lax.axis_index(n) for n in (*W, *F[:1], "zh", "zl")]).astype(jnp.int32)
    up_start = adapter_b[0].T
    group = 2 * lax.axis_index("yl") + lax.axis_index("zl")
    z = lax.axis_index("zh")
    block = lax.dynamic_slice(up_start, (16 * group + 8 * (z // 4), 128 * (z % 4)), (8, 128))

    own, to_y, to_z, to_both = pack(idx, tokens)
    xs = (own, swap(to_y, "yl"), swap(to_z, "zl"), swap_both(to_both))
    cols = gather_z(base.T.astype(bf16))
    cols = cols.transpose(1, 0, 2).reshape(cols.shape[1], width // 4)
    pair = jnp.stack([cols, swap(cols, "yh")])
    near = [pair] + [shift(pair, "x", d, 4) for d in (1, 2, 3)]
    whole = gather_z(a_start.astype(bf16))
    pieces = near + [swap(piece, "c") for piece in near]

    keys_shape = shaped((rows, 512), bf16)
    error_shape = shaped((4, 48, 512), bf16)
    down_shape = shaped((NZ, 72, 256), bf16)

    def gradients(step, mine):
        shared = exchange(mine, Q)
        return exchange(with_tokens(down_kernel, step, down_shape, idx, (shared,), xs), "zh")

    keys = keys_of(0, scale, idx, xs, whole, targets[0], pieces, shaped((4, rows + 32, 512), bf16))
    parts = exchange(keys, Q)
    mine = call(lambda *refs: first_error_kernel(total_rows, *refs), error_shape, parts, up_start)
    parts = gradients(0, mine)

    keys = keys_of(1, scale, idx, xs, whole, targets[0], pieces, [keys_shape] * 4)
    keys = (keys[0], swap(keys[1], "yl"), swap(keys[2], "zl"), swap_both(keys[3]))
    a_next, block, copies = call(
        lambda *refs: update_kernel(scale, *refs),
        (shaped((64, 256), f32), shaped((8, 128), f32), down_shape),
        parts,
        a_start,
        block,
    )
    whole = exchange(copies, "zh")
    low = with_tokens(
        lambda *refs: low_kernel(scale, *refs), 1, shaped((4, 128, 256), bf16), idx, (whole,), xs
    )
    low = exchange(low, Q)
    mine = call(lambda *refs: second_error_kernel(total_rows, *refs), error_shape, low, *keys)
    parts = gradients(1, mine)
    a_last, copies = call(
        lambda *refs: last_update_kernel(scale, *refs),
        (shaped((64, 256), f32), shaped((4 * NZ, 8, 128), f32)),
        parts,
        a_next,
        block,
    )
    blocks = exchange(copies, F)
    change, b_last = call(
        change_kernel, (shaped((512, 256), f32), shaped((64, 512), f32)), a_last, blocks, a_start, up_start
    )
    merged = exchange(change.reshape(16, 32, 256), W)
    new_base = call(merge_kernel, shaped(base.shape[::-1], f32), merged, base.T)
    return (new_base.T, a_last[None], b_last.T[None])


def solution(mesh):
    finer = Mesh(mesh.devices.reshape(4, 2, 2, 2, NZ, 2), (*W, *F))
    return jax.shard_map(
        whole_step,
        mesh=finer,
        in_specs=(
            P(W, None, F, None),
            P(W, None, F, None),
            P(F, W),
            P(W, None, F),
            P(W, None, None),
        ),
        out_specs=(P(F, W), P(W, None, F), P(W, None, None)),
        check_vma=False,
    )
```

```python
import jax
import jax.numpy as jnp
from jax import lax
from jax.experimental import pallas as pl
from jax.experimental.pallas import tpu as pltpu
from jax.sharding import Mesh
from jax.sharding import PartitionSpec as P

W = ("x", "yh", "c")
F = ("yl", "zh", "zl")
Q = ("yl", "zl")
NZ = 8


branch_scale = 0.25
rate_down = 200.0
rate_up = 20.0

bf16 = jnp.bfloat16
f32 = jnp.float32
HIGH = lax.Precision.HIGHEST
VMEM = pltpu.CompilerParams(vmem_limit_bytes=60 * 1024 * 1024)


def dot(a, b, ca, cb, precision=None):
    return lax.dot_general(a, b, (((ca,), (cb,)), ((), ())), precision=precision, preferred_element_type=f32)


def split(value):
    hi = value.astype(bf16)
    return hi, (value - hi.astype(f32)).astype(bf16)


def vmem(n):
    return [pl.BlockSpec(memory_space=pltpu.VMEM)] * n


def smem():
    return pl.BlockSpec(memory_space=pltpu.SMEM)


def pack_kernel(idx, x_ref, *outs):
    yl, zl = idx[3], idx[5]
    n = 256
    for k, out in enumerate(outs):
        start = lax.rem(yl + k % 2, 2) * (2 * NZ * n) + lax.rem(zl + k // 2, 2) * n
        for z in range(NZ):
            out[0, :, z * n : (z + 1) * n] = x_ref[0, :, pl.ds(pl.multiple_of(start + z * 2 * n, n), n)]


def wide(value):
    return jnp.concatenate([value[16 * k : 16 * k + 16] for k in range(4)], axis=1)


def tall(value):
    n = value.shape[1] // 4
    return jnp.concatenate([value[:, k * n : k * n + n] for k in range(4)], axis=0)


def group_at(idx, k):
    return 2 * lax.rem(idx[3] + k % 2, 2) + lax.rem(idx[5] + k // 2, 2)


def partial_low(whole, tokens):
    return dot(jnp.concatenate([whole[z, :64] for z in range(NZ)], axis=1), tokens, 1, 1)


def keys_kernel(step, scale, idx, *rest):
    x_refs, pieces, y_ref, out, bs = rest[:4], rest[4:12], rest[12], rest[-2], rest[-1]
    rows, quarter = x_refs[0].shape[1:]
    px, pyh, pc = idx[0], idx[1], idx[2]
    places = [group_at(idx, k) for k in range(4)]
    tokens = jnp.concatenate([ref[0] for ref in x_refs], axis=0)
    if step == 0:
        low = partial_low(rest[13], tokens) * scale
        for k in range(4):
            hi, lo = split(low[:, k * rows : (k + 1) * rows])
            out[places[k], rows : rows + 16] = wide(hi)
            out[places[k], rows + 16 :] = wide(lo)
    for dx in range(4):
        for dc in range(2):
            for dy in range(2):
                w = lax.rem(pyh + dy, 2) * 2 + lax.rem(pc + dc, 2)
                bs[dx, w] = pieces[4 * dc + dx][dy]
        at = pl.ds(pl.multiple_of(lax.rem(px + 4 - dx, 4) * 128, 128), 128)
        part = dot(tokens, bs[dx].reshape(128, quarter), 1, 1) * scale
        for k in range(4):
            value = part[k * rows : (k + 1) * rows]
            if k == 0:
                value = value - y_ref[0, :, at].astype(f32)
            out[places[k], :rows, at] = value.astype(bf16)


def low_kernel(scale, idx, keys, whole, *rest):
    x_refs, out, held, sem = rest[:4], rest[4], rest[5], rest[6]
    rows = x_refs[0].shape[1]
    low = partial_low(whole, jnp.concatenate([ref[0] for ref in x_refs], axis=0)) * scale
    quarter = jnp.concatenate([whole[z, 64:] for z in range(NZ)], axis=0)
    for k in range(4):
        at = group_at(idx, k)
        hi, lo = split(low[:, k * rows : (k + 1) * rows])
        held[at, :, :128] = hi
        held[at, :, 128:256] = lo
        held[at, :, 256:] = quarter
    copy = pltpu.make_async_copy(held, out.at[:, rows:, :], sem)
    copy.start()
    copy.wait()


def quarter_of(blocks):
    value = blocks[:, :128].astype(f32) + blocks[:, 128:].astype(f32)
    halves = [
        jnp.concatenate([value[8 * (4 * r + c) : 8 * (4 * r + c) + 8] for c in range(4)], axis=1) for r in range(2)
    ]
    return jnp.concatenate(halves, axis=0)


def error_of(total_rows, keys, low, up, out):
    error = (keys + branch_scale * dot(low, up, 0, 0, HIGH)) / total_rows
    back = wide((branch_scale * dot(up, error, 1, 1, HIGH)).astype(bf16))
    hi, lo = split(branch_scale * dot(low, error, 1, 0, HIGH))
    for q in range(4):
        out[q, :16] = back
        out[q, 16:32] = hi[16 * q : 16 * q + 16]
        out[q, 32:] = lo[16 * q : 16 * q + 16]


def first_error_kernel(total_rows, parts, up_ref, out):
    rows = parts.shape[1] - 32
    k = [parts[q, :rows].astype(f32) for q in range(4)]
    low = [tall(parts[q, rows : rows + 16]).astype(f32) + tall(parts[q, rows + 16 :]).astype(f32) for q in range(4)]
    error_of(total_rows, (k[0] + k[1]) + (k[2] + k[3]), (low[0] + low[1]) + (low[2] + low[3]), up_ref[...], out)


def second_error_kernel(total_rows, parts, out, up_out):
    rows = parts.shape[1] - 64
    k = [parts[q, :rows].astype(f32) for q in range(4)]
    low = [parts[q, rows:, :128].astype(f32) + parts[q, rows:, 128:256].astype(f32) for q in range(4)]
    up = jnp.concatenate([quarter_of(parts[q, rows:, 256:]) for q in range(4)], axis=0)
    up_out[...] = up
    error_of(total_rows, (k[0] + k[1]) + (k[2] + k[3]), (low[0] + low[1]) + (low[2] + low[3]), up, out)


def down_kernel(whole_quarter, idx, parts, *rest):
    x_refs, out = rest[:4], rest[4]
    back = jnp.concatenate([tall(parts[group_at(idx, k), :16]) for k in range(4)], axis=1)
    grads = [parts[q, 16:32].astype(f32) + parts[q, 32:].astype(f32) for q in range(4)]
    hi, lo = split((grads[0] + grads[1]) + (grads[2] + grads[3]))
    tokens = jnp.concatenate([ref[0] for ref in x_refs], axis=0)
    n = out.shape[2]
    for z in range(NZ):
        out[z, :64] = dot(back, tokens[:, z * n : (z + 1) * n], 1, 0).astype(bf16)
        r, c = z // 4, z % 4
        if whole_quarter:
            out[z, 64:80] = hi[:, :n]
            out[z, 80:96] = hi[:, n:]
        else:
            out[z, 64:, :128] = hi[8 * r : 8 * r + 8, 128 * c : 128 * c + 128]
            out[z, 64:, 128:] = lo[8 * r : 8 * r + 8, 128 * c : 128 * c + 128]


def summed(parts):
    result = parts[0].astype(f32)
    for k in range(1, parts.shape[0]):
        result = result + parts[k].astype(f32)
    return result


def update_kernel(scale, parts, a_ref, b_ref, a_out, copies):
    grads = summed(parts)
    a = a_ref[...] - (rate_down * scale) * grads[:64]
    hi, lo = split(b_ref[...] - rate_up * (grads[64:, :128] + grads[64:, 128:]))
    a_out[...] = a
    a_half = a.astype(bf16)
    for z in range(NZ):
        copies[z, :64] = a_half
        copies[z, 64:, :128] = hi
        copies[z, 64:, 128:] = lo


def last_update_kernel(scale, idx, parts, a_ref, up_ref, a_out, copies):
    grads = summed(parts)
    a_out[...] = a_ref[...] - (rate_down * scale) * grads[:64]
    at = pl.ds(pl.multiple_of(16 * group_at(idx, 0), 16), 16)
    b = up_ref[at, :] - rate_up * jnp.concatenate([grads[64:80], grads[80:96]], axis=1)
    for q in range(4):
        copies[q] = b


def change_kernel(a_ref, quarters, a_start, up_start, out, b_out):
    up = jnp.concatenate([quarters[q] for q in range(4)], axis=0)
    left = jnp.concatenate([up, -up_start[...]], axis=0)
    right = jnp.concatenate([a_ref[...], a_start[...]], axis=0)
    out[...] = (branch_scale * dot(left, right, 0, 0, HIGH)).astype(bf16)
    b_out[...] = up


def merge_kernel(parts, base, out):
    out[...] = base[...] + summed(parts) * (1.0 / parts.shape[0])


def shaped(dims, kind):
    return jax.ShapeDtypeStruct(dims, kind)


def call(kernel, shapes, *args):
    return pl.pallas_call(kernel, out_shape=shapes, in_specs=vmem(len(args)), compiler_params=VMEM)(*args)


def pack(idx, tokens):
    steps, rows, width = tokens.shape
    quarter = width // 4
    return pl.pallas_call(
        pack_kernel,
        out_shape=[shaped((steps, rows, quarter), bf16)] * 4,
        grid_spec=pltpu.PrefetchScalarGridSpec(
            num_scalar_prefetch=1,
            grid=(steps,),
            in_specs=[pl.BlockSpec((1, rows, width), lambda i, s: (i, 0, 0))],
            out_specs=[pl.BlockSpec((1, rows, quarter), lambda i, s: (i, 0, 0))] * 4,
        ),
        compiler_params=VMEM,
    )(idx, tokens)


def with_tokens(kernel, step, shape, idx, args, xs):
    _, rows, quarter = xs[0].shape
    return pl.pallas_call(
        kernel,
        out_shape=shape,
        grid_spec=pltpu.PrefetchScalarGridSpec(
            num_scalar_prefetch=1,
            grid=(1,),
            in_specs=[pl.BlockSpec(a.shape, lambda i, s, n=a.ndim: (0,) * n) for a in args]
            + [pl.BlockSpec((1, rows, quarter), lambda i, s: (step, 0, 0))] * 4,
            out_specs=pl.BlockSpec(shape.shape, lambda i, s, n=len(shape.shape): (0,) * n),
        ),
        compiler_params=VMEM,
    )(idx, *args, *xs)


def keys_of(step, scale, idx, shape, xs, targets, pieces, *more):
    _, rows, quarter = xs[0].shape

    def body(*refs):
        keys_kernel(step, scale, *refs)

    return pl.pallas_call(
        body,
        out_shape=shape,
        grid_spec=pltpu.PrefetchScalarGridSpec(
            num_scalar_prefetch=1,
            grid=(1,),
            in_specs=[pl.BlockSpec((1, rows, quarter), lambda i, s: (step, 0, 0))] * 4
            + [pl.BlockSpec(a.shape, lambda i, s: (0, 0, 0)) for a in pieces]
            + [pl.BlockSpec((1, rows, 512), lambda i, s: (step, 0, 0))]
            + [pl.BlockSpec(a.shape, lambda i, s: (0, 0, 0)) for a in more],
            out_specs=pl.BlockSpec((4, rows + 32 * (1 - step), 512), lambda i, s: (0, 0, 0)),
            scratch_shapes=[pltpu.VMEM((4, 4, 32, quarter), bf16)],
        ),
        compiler_params=VMEM,
    )(idx, *xs, *pieces, targets, *more)


def low_of(scale, idx, keys, whole, xs):
    _, rows, quarter = xs[0].shape

    def body(*refs):
        low_kernel(scale, *refs)

    return pl.pallas_call(
        body,
        out_shape=shaped(keys.shape, bf16),
        grid_spec=pltpu.PrefetchScalarGridSpec(
            num_scalar_prefetch=1,
            grid=(1,),
            in_specs=[pl.BlockSpec(memory_space=pl.ANY), pl.BlockSpec(whole.shape, lambda i, s: (0, 0, 0))]
            + [pl.BlockSpec((1, rows, quarter), lambda i, s: (1, 0, 0))] * 4,
            out_specs=pl.BlockSpec(memory_space=pl.ANY),
            scratch_shapes=[pltpu.VMEM((4, 64, 512), bf16), pltpu.SemaphoreType.DMA],
        ),
        input_output_aliases={1: 0},
        compiler_params=VMEM,
    )(idx, keys, whole, *xs)


def swap(value, axis):
    return lax.ppermute(value, axis, [(0, 1), (1, 0)])


def swap_both(value):
    return lax.ppermute(value, Q, [(k, 3 - k) for k in range(4)])


def shift(value, axis, by, count):
    return lax.ppermute(value, axis, [(i, (i + by) % count) for i in range(count)])


def exchange(parts, axis):
    return lax.all_to_all(parts, axis, 0, 0, tiled=True)


def gather_z(value):
    return exchange(jnp.broadcast_to(value, (NZ, *value.shape)), "zh")


def whole_step(inputs, targets, base, adapter_a, adapter_b):
    tokens = inputs[0]
    a_start = adapter_a[0]
    _, rows, width = tokens.shape
    scale = width ** (-0.5)
    total_rows = float(rows * 4 * NZ)
    idx = jnp.stack([lax.axis_index(n) for n in (*W, *F[:1], "zh", "zl")]).astype(jnp.int32)
    up_start = adapter_b[0].T
    group = 2 * lax.axis_index("yl") + lax.axis_index("zl")
    z = lax.axis_index("zh")
    block = lax.dynamic_slice(up_start, (16 * group + 8 * (z // 4), 128 * (z % 4)), (8, 128))

    own, to_y, to_z, to_both = pack(idx, tokens)
    xs = (own, swap(to_y, "yl"), swap(to_z, "zl"), swap_both(to_both))
    cols = gather_z(base.T.astype(bf16))
    cols = cols.transpose(1, 0, 2).reshape(cols.shape[1], width // 4)
    pair = jnp.stack([cols, swap(cols, "yh")])
    near = [pair] + [shift(pair, "x", d, 4) for d in (1, 2, 3)]
    whole = gather_z(a_start.astype(bf16))
    pieces = near + [swap(piece, "c") for piece in near]

    error_shape = shaped((4, 48, 512), bf16)

    def gradients(step, mine):
        shared = exchange(mine, Q)

        def body(*refs):
            down_kernel(step == 1, *refs)

        shape = shaped((NZ, 96 if step else 72, 256), bf16)
        return exchange(with_tokens(body, step, shape, idx, (shared,), xs), "zh")

    keys = keys_of(0, scale, idx, shaped((4, rows + 32, 512), bf16), xs, targets[0], pieces, whole)
    parts = exchange(keys, Q)
    mine = call(lambda *refs: first_error_kernel(total_rows, *refs), error_shape, parts, up_start)
    parts = gradients(0, mine)

    keys = keys_of(1, scale, idx, shaped((4, rows + 64, 512), bf16), xs, targets[0], pieces)
    a_next, copies = call(
        lambda *refs: update_kernel(scale, *refs),
        (shaped((64, 256), f32), shaped((NZ, 72, 256), bf16)),
        parts,
        a_start,
        block,
    )
    whole = exchange(copies, "zh")
    low = exchange(low_of(scale, idx, keys, whole, xs), Q)
    mine, up_next = call(
        lambda *refs: second_error_kernel(total_rows, *refs), (error_shape, shaped((64, 512), f32)), low
    )
    parts = gradients(1, mine)
    a_last, copies = pl.pallas_call(
        lambda *refs: last_update_kernel(scale, *refs),
        out_shape=(shaped((64, 256), f32), shaped((4, 16, 512), f32)),
        in_specs=[smem()] + vmem(3),
        compiler_params=VMEM,
    )(idx, parts, a_next, up_next)
    quarters = exchange(copies, Q)
    change, b_last = call(
        change_kernel, (shaped((512, 256), bf16), shaped((64, 512), f32)), a_last, quarters, a_start, up_start
    )
    merged = exchange(change.reshape(16, 32, 256), W)
    new_base = call(merge_kernel, shaped(base.shape[::-1], f32), merged, base.T)
    return (new_base.T, a_last[None], b_last.T[None])


def solution(mesh):
    finer = Mesh(mesh.devices.reshape(4, 2, 2, 2, NZ, 2), (*W, *F))
    return jax.shard_map(
        whole_step,
        mesh=finer,
        in_specs=(
            P(W, None, F, None),
            P(W, None, F, None),
            P(F, W),
            P(W, None, F),
            P(W, None, None),
        ),
        out_specs=(P(F, W), P(W, None, F), P(W, None, None)),
        check_vma=False,
    )
```

```python
import jax
import jax.numpy as jnp
from jax import lax
from jax.experimental import pallas as pl
from jax.experimental.pallas import tpu as pltpu
from jax.sharding import Mesh
from jax.sharding import PartitionSpec as P

W = ("x", "yh", "c")
F = ("yl", "zh", "zl")
Q = ("yl", "zl")
NZ = 8


branch_scale = 0.25
rate_down = 200.0
rate_up = 20.0

bf16 = jnp.bfloat16
f32 = jnp.float32
HIGH = lax.Precision.HIGHEST
VMEM = pltpu.CompilerParams(vmem_limit_bytes=60 * 1024 * 1024)


def dot(a, b, ca, cb, precision=None):
    return lax.dot_general(a, b, (((ca,), (cb,)), ((), ())), precision=precision, preferred_element_type=f32)


def split(value):
    hi = value.astype(bf16)
    return hi, (value - hi.astype(f32)).astype(bf16)


def vmem(n):
    return [pl.BlockSpec(memory_space=pltpu.VMEM)] * n


def smem():
    return pl.BlockSpec(memory_space=pltpu.SMEM)


def start_kernel(base, a_ref, out):
    for z in range(NZ):
        out[z, :32] = base[...].astype(bf16)
        out[z, 32:] = a_ref[...].astype(bf16)


def pack_kernel(idx, x_ref, own, to_y, to_z0, to_z1, to_both0, to_both1):
    yl, zl = idx[3], idx[5]
    n = 256
    for k, outs in enumerate(((own,), (to_y,), (to_z0, to_z1), (to_both0, to_both1))):
        start = lax.rem(yl + k % 2, 2) * (2 * NZ * n) + lax.rem(zl + k // 2, 2) * n
        for step in range(2):
            out = outs[0].at[step] if len(outs) == 1 else outs[step].at[0]
            for z in range(NZ):
                out[:, z * n : (z + 1) * n] = x_ref[step, :, pl.ds(pl.multiple_of(start + z * 2 * n, n), n)]


def wide(value):
    return jnp.concatenate([value[16 * k : 16 * k + 16] for k in range(4)], axis=1)


def tall(value):
    n = value.shape[1] // 4
    return jnp.concatenate([value[:, k * n : k * n + n] for k in range(4)], axis=0)


def group_at(idx, k):
    return 2 * lax.rem(idx[3] + k % 2, 2) + lax.rem(idx[5] + k // 2, 2)


def keys_kernel(step, scale, idx, *rest):
    x_refs, pieces, y_ref, out, bs = rest[:4], rest[4:6], rest[6], rest[-2], rest[-1]
    rows, quarter = x_refs[0].shape[1:]
    places = [group_at(idx, k) for k in range(4)]
    tokens = jnp.concatenate([ref[0] for ref in x_refs], axis=0)
    if step == 0:
        whole = rest[7]
        a_half = jnp.concatenate([whole[z, 32:] for z in range(NZ)], axis=1)
        low = dot(a_half, tokens, 1, 1) * scale
        for k in range(4):
            hi, lo = split(low[:, k * rows : (k + 1) * rows])
            out[places[k], rows : rows + 16] = wide(hi)
            out[places[k], rows + 16 :] = wide(lo)
    for x in range(4):
        for dc in range(2):
            for y in range(2):
                bs[x, 2 * y + lax.rem(idx[2] + dc, 2)] = pieces[dc][2 * x + y]
        at = slice(x * 128, x * 128 + 128)
        part = dot(tokens, bs[x].reshape(128, quarter), 1, 1) * scale
        for k in range(4):
            value = part[k * rows : (k + 1) * rows]
            if k == 0:
                value = value - y_ref[0, :, at].astype(f32)
            out[places[k], :rows, at] = value.astype(bf16)


def low_kernel(scale, idx, keys, whole, *rest):
    x_refs, out, held, sem = rest[:4], rest[4], rest[5], rest[6]
    rows = x_refs[0].shape[1]
    a_half = jnp.concatenate([whole[z, :64] for z in range(NZ)], axis=1)
    low = dot(a_half, jnp.concatenate([ref[0] for ref in x_refs], axis=0), 1, 1) * scale
    quarter = jnp.concatenate([whole[z, 64:] for z in range(NZ)], axis=0)
    for k in range(4):
        at = group_at(idx, k)
        hi, lo = split(low[:, k * rows : (k + 1) * rows])
        held[at, :, :128] = hi
        held[at, :, 128:256] = lo
        held[at, :, 256:] = quarter
    copy = pltpu.make_async_copy(held, out.at[:, rows:, :], sem)
    copy.start()
    copy.wait()


def quarter_of(blocks):
    value = blocks[:, :128].astype(f32) + blocks[:, 128:].astype(f32)
    halves = [
        jnp.concatenate([value[8 * (4 * r + c) : 8 * (4 * r + c) + 8] for c in range(4)], axis=1) for r in range(2)
    ]
    return jnp.concatenate(halves, axis=0)


def error_of(total_rows, keys, low, up, out):
    error = (keys + branch_scale * dot(low, up, 0, 0, HIGH)) / total_rows
    back = wide((branch_scale * dot(up, error, 1, 1, HIGH)).astype(bf16))
    hi, lo = split(branch_scale * dot(low, error, 1, 0, HIGH))
    for q in range(4):
        out[q, :16] = back
        out[q, 16:32] = hi[16 * q : 16 * q + 16]
        out[q, 32:] = lo[16 * q : 16 * q + 16]


def first_error_kernel(total_rows, parts, up_ref, out):
    rows = parts.shape[1] - 32
    k = [parts[q, :rows].astype(f32) for q in range(4)]
    low = [tall(parts[q, rows : rows + 16]).astype(f32) + tall(parts[q, rows + 16 :]).astype(f32) for q in range(4)]
    error_of(total_rows, (k[0] + k[1]) + (k[2] + k[3]), (low[0] + low[1]) + (low[2] + low[3]), up_ref[...], out)


def second_error_kernel(total_rows, parts, out, up_out):
    rows = parts.shape[1] - 64
    k = [parts[q, :rows].astype(f32) for q in range(4)]
    low = [parts[q, rows:, :128].astype(f32) + parts[q, rows:, 128:256].astype(f32) for q in range(4)]
    up = jnp.concatenate([quarter_of(parts[q, rows:, 256:]) for q in range(4)], axis=0)
    up_out[...] = up
    error_of(total_rows, (k[0] + k[1]) + (k[2] + k[3]), (low[0] + low[1]) + (low[2] + low[3]), up, out)


def down_kernel(whole_quarter, idx, parts, *rest):
    x_refs, out = rest[:4], rest[4]
    back = jnp.concatenate([tall(parts[group_at(idx, k), :16]) for k in range(4)], axis=1)
    grads = [parts[q, 16:32].astype(f32) + parts[q, 32:].astype(f32) for q in range(4)]
    hi, lo = split((grads[0] + grads[1]) + (grads[2] + grads[3]))
    tokens = jnp.concatenate([ref[0] for ref in x_refs], axis=0)
    n = out.shape[2]
    for z in range(NZ):
        out[z, :64] = dot(back, tokens[:, z * n : (z + 1) * n], 1, 0).astype(bf16)
        r, c = z // 4, z % 4
        if whole_quarter:
            out[z, 64:80] = hi[:, :n]
            out[z, 80:96] = hi[:, n:]
        else:
            out[z, 64:, :128] = hi[8 * r : 8 * r + 8, 128 * c : 128 * c + 128]
            out[z, 64:, 128:] = lo[8 * r : 8 * r + 8, 128 * c : 128 * c + 128]


def summed(parts):
    result = parts[0].astype(f32)
    for k in range(1, parts.shape[0]):
        result = result + parts[k].astype(f32)
    return result


def update_kernel(scale, parts, a_ref, b_ref, a_out, copies):
    grads = summed(parts)
    a = a_ref[...] - (rate_down * scale) * grads[:64]
    hi, lo = split(b_ref[...] - rate_up * (grads[64:, :128] + grads[64:, 128:]))
    a_out[...] = a
    a_half = a.astype(bf16)
    for z in range(NZ):
        copies[z, :64] = a_half
        copies[z, 64:, :128] = hi
        copies[z, 64:, 128:] = lo


def last_update_kernel(scale, idx, parts, a_ref, up_ref, a_out, copies):
    grads = summed(parts)
    a_out[...] = a_ref[...] - (rate_down * scale) * grads[:64]
    at = pl.ds(pl.multiple_of(16 * group_at(idx, 0), 16), 16)
    b = up_ref[at, :] - rate_up * jnp.concatenate([grads[64:80], grads[80:96]], axis=1)
    for q in range(4):
        copies[q] = b


def change_kernel(a_ref, quarters, a_start, up_start, out, b_out):
    up = jnp.concatenate([quarters[q] for q in range(4)], axis=0)
    left = jnp.concatenate([up, -up_start[...]], axis=0)
    right = jnp.concatenate([a_ref[...], a_start[...]], axis=0)
    out[...] = (branch_scale * dot(left, right, 0, 0, HIGH)).astype(bf16)
    b_out[...] = up


def merge_kernel(parts, base, out):
    out[...] = base[...] + summed(parts) * (1.0 / parts.shape[0])


def shaped(dims, kind):
    return jax.ShapeDtypeStruct(dims, kind)


def call(kernel, shapes, *args):
    return pl.pallas_call(kernel, out_shape=shapes, in_specs=vmem(len(args)), compiler_params=VMEM)(*args)


def pack(idx, tokens):
    steps, rows, width = tokens.shape
    both = shaped((steps, rows, width // 4), bf16)
    single = shaped((1, rows, width // 4), bf16)
    return pl.pallas_call(
        pack_kernel,
        out_shape=[both, both] + [single] * 4,
        in_specs=[smem()] + vmem(1),
        compiler_params=VMEM,
    )(idx, tokens)


def token_specs(step, xs):
    return [
        pl.BlockSpec((1, *x.shape[1:]), lambda i, s, at=step if x.shape[0] > 1 else 0: (at, 0, 0)) for x in xs
    ]


def with_tokens(kernel, step, shape, idx, args, xs):
    return pl.pallas_call(
        kernel,
        out_shape=shape,
        grid_spec=pltpu.PrefetchScalarGridSpec(
            num_scalar_prefetch=1,
            grid=(1,),
            in_specs=[pl.BlockSpec(a.shape, lambda i, s, n=a.ndim: (0,) * n) for a in args]
            + token_specs(step, xs),
            out_specs=pl.BlockSpec(shape.shape, lambda i, s, n=len(shape.shape): (0,) * n),
        ),
        compiler_params=VMEM,
    )(idx, *args, *xs)


def keys_of(step, scale, idx, shape, xs, targets, pieces, *more):
    _, rows, quarter = xs[0].shape

    def body(*refs):
        keys_kernel(step, scale, *refs)

    return pl.pallas_call(
        body,
        out_shape=shape,
        grid_spec=pltpu.PrefetchScalarGridSpec(
            num_scalar_prefetch=1,
            grid=(1,),
            in_specs=token_specs(step, xs)
            + [pl.BlockSpec(a.shape, lambda i, s: (0, 0, 0)) for a in pieces]
            + [pl.BlockSpec((1, rows, 512), lambda i, s: (step, 0, 0))]
            + [pl.BlockSpec(a.shape, lambda i, s: (0, 0, 0)) for a in more],
            out_specs=pl.BlockSpec((4, rows + 32 * (1 - step), 512), lambda i, s: (0, 0, 0)),
            scratch_shapes=[pltpu.VMEM((4, 4, 32, quarter), bf16)],
        ),
        compiler_params=VMEM,
    )(idx, *xs, *pieces, targets, *more)


def low_of(scale, idx, keys, whole, xs):
    def body(*refs):
        low_kernel(scale, *refs)

    return pl.pallas_call(
        body,
        out_shape=shaped(keys.shape, bf16),
        grid_spec=pltpu.PrefetchScalarGridSpec(
            num_scalar_prefetch=1,
            grid=(1,),
            in_specs=[pl.BlockSpec(memory_space=pl.ANY), pl.BlockSpec(whole.shape, lambda i, s: (0, 0, 0))]
            + token_specs(1, xs),
            out_specs=pl.BlockSpec(memory_space=pl.ANY),
            scratch_shapes=[pltpu.VMEM((4, 64, 512), bf16), pltpu.SemaphoreType.DMA],
        ),
        input_output_aliases={1: 0},
        compiler_params=VMEM,
    )(idx, keys, whole, *xs)


def swap(value, axis):
    return lax.ppermute(value, axis, [(0, 1), (1, 0)])


def swap_both(value):
    return lax.ppermute(value, Q, [(k, 3 - k) for k in range(4)])


def exchange(parts, axis):
    return lax.all_to_all(parts, axis, 0, 0, tiled=True)


def whole_step(inputs, targets, base, adapter_a, adapter_b):
    tokens = inputs[0]
    a_start = adapter_a[0]
    _, rows, width = tokens.shape
    scale = width ** (-0.5)
    total_rows = float(rows * 4 * NZ)
    idx = jnp.stack([lax.axis_index(n) for n in (*W, *F[:1], "zh", "zl")]).astype(jnp.int32)
    up_start = adapter_b[0].T
    group = 2 * lax.axis_index("yl") + lax.axis_index("zl")
    z = lax.axis_index("zh")
    block = lax.dynamic_slice(up_start, (16 * group + 8 * (z // 4), 128 * (z % 4)), (8, 128))

    own, to_y, *rest = pack(idx, tokens)
    by_y = swap(to_y, "yl")
    xs = [(own, by_y, swap(rest[j], "zl"), swap_both(rest[2 + j])) for j in range(2)]
    whole = exchange(call(start_kernel, shaped((NZ, 96, 256), bf16), base.T, a_start), "zh")
    cols = whole[:, :32].transpose(1, 0, 2).reshape(32, width // 4)
    near = exchange(jnp.broadcast_to(cols, (8, *cols.shape)), ("x", "yh"))
    pieces = (near, swap(near, "c"))

    error_shape = shaped((4, 48, 512), bf16)

    def gradients(step, mine):
        shared = exchange(mine, Q)

        def body(*refs):
            down_kernel(step == 1, *refs)

        shape = shaped((NZ, 96 if step else 72, 256), bf16)
        return exchange(with_tokens(body, step, shape, idx, (shared,), xs[step]), "zh")

    keys = keys_of(0, scale, idx, shaped((4, rows + 32, 512), bf16), xs[0], targets[0], pieces, whole)
    parts = exchange(keys, Q)
    mine = call(lambda *refs: first_error_kernel(total_rows, *refs), error_shape, parts, up_start)
    parts = gradients(0, mine)

    keys = keys_of(1, scale, idx, shaped((4, rows + 64, 512), bf16), xs[1], targets[0], pieces)
    a_next, copies = call(
        lambda *refs: update_kernel(scale, *refs),
        (shaped((64, 256), f32), shaped((NZ, 72, 256), bf16)),
        parts,
        a_start,
        block,
    )
    whole = exchange(copies, "zh")
    low = exchange(low_of(scale, idx, keys, whole, xs[1]), Q)
    mine, up_next = call(
        lambda *refs: second_error_kernel(total_rows, *refs), (error_shape, shaped((64, 512), f32)), low
    )
    parts = gradients(1, mine)
    a_last, copies = pl.pallas_call(
        lambda *refs: last_update_kernel(scale, *refs),
        out_shape=(shaped((64, 256), f32), shaped((4, 16, 512), f32)),
        in_specs=[smem()] + vmem(3),
        compiler_params=VMEM,
    )(idx, parts, a_next, up_next)
    quarters = exchange(copies, Q)
    change, b_last = call(
        change_kernel, (shaped((512, 256), bf16), shaped((64, 512), f32)), a_last, quarters, a_start, up_start
    )
    merged = exchange(change.reshape(16, 32, 256), W)
    new_base = call(merge_kernel, shaped(base.shape[::-1], f32), merged, base.T)
    return (new_base.T, a_last[None], b_last.T[None])


def solution(mesh):
    finer = Mesh(mesh.devices.reshape(4, 2, 2, 2, NZ, 2), (*W, *F))
    return jax.shard_map(
        whole_step,
        mesh=finer,
        in_specs=(
            P(W, None, F, None),
            P(W, None, F, None),
            P(F, W),
            P(W, None, F),
            P(W, None, None),
        ),
        out_specs=(P(F, W), P(W, None, F), P(W, None, None)),
        check_vma=False,
    )
```

```python
import jax
import jax.numpy as jnp
from jax import lax
from jax.experimental import pallas as pl
from jax.experimental.pallas import tpu as pltpu
from jax.sharding import Mesh
from jax.sharding import PartitionSpec as P

W = ("x", "yh", "c")
F = ("yl", "zh", "zl")
Q = ("yl", "zl")
NZ = 8


branch_scale = 0.25
rate_down = 200.0
rate_up = 20.0

bf16 = jnp.bfloat16
f32 = jnp.float32
HIGH = lax.Precision.HIGHEST
VMEM = pltpu.CompilerParams(vmem_limit_bytes=60 * 1024 * 1024)


def dot(a, b, ca, cb, precision=None):
    return lax.dot_general(a, b, (((ca,), (cb,)), ((), ())), precision=precision, preferred_element_type=f32)


def split(value):
    hi = value.astype(bf16)
    return hi, (value - hi.astype(f32)).astype(bf16)


def vmem(n):
    return [pl.BlockSpec(memory_space=pltpu.VMEM)] * n


def smem():
    return pl.BlockSpec(memory_space=pltpu.SMEM)


def start_kernel(base, a_ref, out):
    for z in range(NZ):
        out[z, :32] = base[...].astype(bf16)
        out[z, 32:] = a_ref[...].astype(bf16)


def pack_kernel(idx, x_ref, *outs):
    yl, zl = idx[3], idx[5]
    n = 256
    for k, out in enumerate(outs):
        start = lax.rem(yl + k % 2, 2) * (2 * NZ * n) + lax.rem(zl + k // 2, 2) * n
        for z in range(NZ):
            out[0, :, z * n : (z + 1) * n] = x_ref[0, :, pl.ds(pl.multiple_of(start + z * 2 * n, n), n)]


def wide(value):
    return jnp.concatenate([value[16 * k : 16 * k + 16] for k in range(4)], axis=1)


def tall(value):
    n = value.shape[1] // 4
    return jnp.concatenate([value[:, k * n : k * n + n] for k in range(4)], axis=0)


def group_at(idx, k):
    return 2 * lax.rem(idx[3] + k % 2, 2) + lax.rem(idx[5] + k // 2, 2)


def keys_kernel(step, scale, idx, *rest):
    x_refs, pieces, y_ref, out, bs = rest[:4], rest[4:6], rest[6], rest[-2], rest[-1]
    rows, quarter = x_refs[0].shape[1:]
    places = [group_at(idx, k) for k in range(4)]
    tokens = jnp.concatenate([ref[0] for ref in x_refs], axis=0)
    if step == 0:
        whole = rest[7]
        a_half = jnp.concatenate([whole[z, 32:] for z in range(NZ)], axis=1)
        low = dot(a_half, tokens, 1, 1) * scale
        for k in range(4):
            hi, lo = split(low[:, k * rows : (k + 1) * rows])
            out[places[k], rows : rows + 16] = wide(hi)
            out[places[k], rows + 16 :] = wide(lo)
    for x in range(4):
        for dc in range(2):
            for y in range(2):
                bs[x, 2 * y + lax.rem(idx[2] + dc, 2)] = pieces[dc][2 * x + y]
        at = slice(x * 128, x * 128 + 128)
        part = dot(tokens, bs[x].reshape(128, quarter), 1, 1) * scale
        for k in range(4):
            value = part[k * rows : (k + 1) * rows]
            if k == 0:
                value = value - y_ref[0, :, at].astype(f32)
            out[places[k], :rows, at] = value.astype(bf16)


def low_kernel(scale, idx, keys, whole, *rest):
    x_refs, out, held, sem = rest[:4], rest[4], rest[5], rest[6]
    rows = x_refs[0].shape[1]
    a_half = jnp.concatenate([whole[z, :64] for z in range(NZ)], axis=1)
    low = dot(a_half, jnp.concatenate([ref[0] for ref in x_refs], axis=0), 1, 1) * scale
    quarter = jnp.concatenate([whole[z, 64:] for z in range(NZ)], axis=0)
    for k in range(4):
        at = group_at(idx, k)
        hi, lo = split(low[:, k * rows : (k + 1) * rows])
        held[at, :, :128] = hi
        held[at, :, 128:256] = lo
        held[at, :, 256:] = quarter
    copy = pltpu.make_async_copy(held, out.at[:, rows:, :], sem)
    copy.start()
    copy.wait()


def quarter_of(blocks):
    value = blocks[:, :128].astype(f32) + blocks[:, 128:].astype(f32)
    halves = [
        jnp.concatenate([value[8 * (4 * r + c) : 8 * (4 * r + c) + 8] for c in range(4)], axis=1) for r in range(2)
    ]
    return jnp.concatenate(halves, axis=0)


def error_of(total_rows, keys, low, up, out):
    error = (keys + branch_scale * dot(low, up, 0, 0, HIGH)) / total_rows
    back = wide((branch_scale * dot(up, error, 1, 1, HIGH)).astype(bf16))
    hi, lo = split(branch_scale * dot(low, error, 1, 0, HIGH))
    for q in range(4):
        out[q, :16] = back
        out[q, 16:32] = hi[16 * q : 16 * q + 16]
        out[q, 32:] = lo[16 * q : 16 * q + 16]


def first_error_kernel(total_rows, parts, up_ref, out):
    rows = parts.shape[1] - 32
    k = [parts[q, :rows].astype(f32) for q in range(4)]
    low = [tall(parts[q, rows : rows + 16]).astype(f32) + tall(parts[q, rows + 16 :]).astype(f32) for q in range(4)]
    error_of(total_rows, (k[0] + k[1]) + (k[2] + k[3]), (low[0] + low[1]) + (low[2] + low[3]), up_ref[...], out)


def second_error_kernel(total_rows, parts, out, up_out):
    rows = parts.shape[1] - 64
    k = [parts[q, :rows].astype(f32) for q in range(4)]
    low = [parts[q, rows:, :128].astype(f32) + parts[q, rows:, 128:256].astype(f32) for q in range(4)]
    up = jnp.concatenate([quarter_of(parts[q, rows:, 256:]) for q in range(4)], axis=0)
    up_out[...] = up
    error_of(total_rows, (k[0] + k[1]) + (k[2] + k[3]), (low[0] + low[1]) + (low[2] + low[3]), up, out)


def down_kernel(whole_quarter, idx, parts, *rest):
    x_refs, out = rest[:4], rest[4]
    back = jnp.concatenate([tall(parts[group_at(idx, k), :16]) for k in range(4)], axis=1)
    grads = [parts[q, 16:32].astype(f32) + parts[q, 32:].astype(f32) for q in range(4)]
    hi, lo = split((grads[0] + grads[1]) + (grads[2] + grads[3]))
    tokens = jnp.concatenate([ref[0] for ref in x_refs], axis=0)
    n = out.shape[2]
    for z in range(NZ):
        out[z, :64] = dot(back, tokens[:, z * n : (z + 1) * n], 1, 0).astype(bf16)
        r, c = z // 4, z % 4
        if whole_quarter:
            out[z, 64:80] = hi[:, :n]
            out[z, 80:96] = hi[:, n:]
        else:
            out[z, 64:, :128] = hi[8 * r : 8 * r + 8, 128 * c : 128 * c + 128]
            out[z, 64:, 128:] = lo[8 * r : 8 * r + 8, 128 * c : 128 * c + 128]


def summed(parts):
    result = parts[0].astype(f32)
    for k in range(1, parts.shape[0]):
        result = result + parts[k].astype(f32)
    return result


def update_kernel(scale, parts, a_ref, b_ref, a_out, copies):
    grads = summed(parts)
    a = a_ref[...] - (rate_down * scale) * grads[:64]
    hi, lo = split(b_ref[...] - rate_up * (grads[64:, :128] + grads[64:, 128:]))
    a_out[...] = a
    a_half = a.astype(bf16)
    for z in range(NZ):
        copies[z, :64] = a_half
        copies[z, 64:, :128] = hi
        copies[z, 64:, 128:] = lo


def last_update_kernel(scale, idx, parts, a_ref, up_ref, a_out, copies):
    grads = summed(parts)
    a_out[...] = a_ref[...] - (rate_down * scale) * grads[:64]
    at = pl.ds(pl.multiple_of(16 * group_at(idx, 0), 16), 16)
    b = up_ref[at, :] - rate_up * jnp.concatenate([grads[64:80], grads[80:96]], axis=1)
    for q in range(4):
        copies[q] = b


def change_kernel(a_ref, quarters, a_start, up_start, out, b_out):
    up = jnp.concatenate([quarters[q] for q in range(4)], axis=0)
    left = jnp.concatenate([up, -up_start[...]], axis=0)
    right = jnp.concatenate([a_ref[...], a_start[...]], axis=0)
    out[...] = (branch_scale * dot(left, right, 0, 0, HIGH)).astype(bf16)
    b_out[...] = up


def merge_kernel(parts, base, out):
    out[...] = base[...] + summed(parts) * (1.0 / parts.shape[0])


def shaped(dims, kind):
    return jax.ShapeDtypeStruct(dims, kind)


def call(kernel, shapes, *args):
    return pl.pallas_call(kernel, out_shape=shapes, in_specs=vmem(len(args)), compiler_params=VMEM)(*args)


def pack(idx, tokens):
    steps, rows, width = tokens.shape
    quarter = width // 4
    return pl.pallas_call(
        pack_kernel,
        out_shape=[shaped((steps, rows, quarter), bf16)] * 4,
        grid_spec=pltpu.PrefetchScalarGridSpec(
            num_scalar_prefetch=1,
            grid=(steps,),
            in_specs=[pl.BlockSpec((1, rows, width), lambda i, s: (i, 0, 0))],
            out_specs=[pl.BlockSpec((1, rows, quarter), lambda i, s: (i, 0, 0))] * 4,
        ),
        compiler_params=VMEM,
    )(idx, tokens)


def token_specs(step, xs):
    return [pl.BlockSpec((1, *x.shape[1:]), lambda i, s: (step, 0, 0)) for x in xs]


def with_tokens(kernel, step, shape, idx, args, xs):
    return pl.pallas_call(
        kernel,
        out_shape=shape,
        grid_spec=pltpu.PrefetchScalarGridSpec(
            num_scalar_prefetch=1,
            grid=(1,),
            in_specs=[pl.BlockSpec(a.shape, lambda i, s, n=a.ndim: (0,) * n) for a in args]
            + token_specs(step, xs),
            out_specs=pl.BlockSpec(shape.shape, lambda i, s, n=len(shape.shape): (0,) * n),
        ),
        compiler_params=VMEM,
    )(idx, *args, *xs)


def keys_of(step, scale, idx, shape, xs, targets, pieces, *more):
    _, rows, quarter = xs[0].shape

    def body(*refs):
        keys_kernel(step, scale, *refs)

    return pl.pallas_call(
        body,
        out_shape=shape,
        grid_spec=pltpu.PrefetchScalarGridSpec(
            num_scalar_prefetch=1,
            grid=(1,),
            in_specs=token_specs(step, xs)
            + [pl.BlockSpec(a.shape, lambda i, s: (0, 0, 0)) for a in pieces]
            + [pl.BlockSpec((1, rows, 512), lambda i, s: (step, 0, 0))]
            + [pl.BlockSpec(a.shape, lambda i, s: (0, 0, 0)) for a in more],
            out_specs=pl.BlockSpec((4, rows + 32 * (1 - step), 512), lambda i, s: (0, 0, 0)),
            scratch_shapes=[pltpu.VMEM((4, 4, 32, quarter), bf16)],
        ),
        compiler_params=VMEM,
    )(idx, *xs, *pieces, targets, *more)


def low_of(scale, idx, keys, whole, xs):
    def body(*refs):
        low_kernel(scale, *refs)

    return pl.pallas_call(
        body,
        out_shape=shaped(keys.shape, bf16),
        grid_spec=pltpu.PrefetchScalarGridSpec(
            num_scalar_prefetch=1,
            grid=(1,),
            in_specs=[pl.BlockSpec(memory_space=pl.ANY), pl.BlockSpec(whole.shape, lambda i, s: (0, 0, 0))]
            + token_specs(1, xs),
            out_specs=pl.BlockSpec(memory_space=pl.ANY),
            scratch_shapes=[pltpu.VMEM((4, 64, 512), bf16), pltpu.SemaphoreType.DMA],
        ),
        input_output_aliases={1: 0},
        compiler_params=VMEM,
    )(idx, keys, whole, *xs)


def swap(value, axis):
    return lax.ppermute(value, axis, [(0, 1), (1, 0)])


def swap_both(value):
    return lax.ppermute(value, Q, [(k, 3 - k) for k in range(4)])


def exchange(parts, axis):
    return lax.all_to_all(parts, axis, 0, 0, tiled=True)


def whole_step(inputs, targets, base, adapter_a, adapter_b):
    tokens = inputs[0]
    a_start = adapter_a[0]
    _, rows, width = tokens.shape
    scale = width ** (-0.5)
    total_rows = float(rows * 4 * NZ)
    idx = jnp.stack([lax.axis_index(n) for n in (*W, *F[:1], "zh", "zl")]).astype(jnp.int32)
    up_start = adapter_b[0].T
    group = 2 * lax.axis_index("yl") + lax.axis_index("zl")
    z = lax.axis_index("zh")
    block = lax.dynamic_slice(up_start, (16 * group + 8 * (z // 4), 128 * (z % 4)), (8, 128))

    own, to_y, to_z, to_both = pack(idx, tokens)
    xs = (own, swap(to_y, "yl"), swap(to_z, "zl"), swap_both(to_both))
    whole = exchange(call(start_kernel, shaped((NZ, 96, 256), bf16), base.T, a_start), "zh")
    cols = whole[:, :32].transpose(1, 0, 2).reshape(32, width // 4)
    near = exchange(jnp.broadcast_to(cols, (8, *cols.shape)), ("x", "yh"))
    pieces = (near, swap(near, "c"))

    error_shape = shaped((4, 48, 512), bf16)

    def gradients(step, mine):
        shared = exchange(mine, Q)

        def body(*refs):
            down_kernel(step == 1, *refs)

        shape = shaped((NZ, 96 if step else 72, 256), bf16)
        return exchange(with_tokens(body, step, shape, idx, (shared,), xs), "zh")

    keys = keys_of(0, scale, idx, shaped((4, rows + 32, 512), bf16), xs, targets[0], pieces, whole)
    parts = exchange(keys, Q)
    mine = call(lambda *refs: first_error_kernel(total_rows, *refs), error_shape, parts, up_start)
    parts = gradients(0, mine)

    keys = keys_of(1, scale, idx, shaped((4, rows + 64, 512), bf16), xs, targets[0], pieces)
    a_next, copies = call(
        lambda *refs: update_kernel(scale, *refs),
        (shaped((64, 256), f32), shaped((NZ, 72, 256), bf16)),
        parts,
        a_start,
        block,
    )
    whole = exchange(copies, "zh")
    low = exchange(low_of(scale, idx, keys, whole, xs), Q)
    mine, up_next = call(
        lambda *refs: second_error_kernel(total_rows, *refs), (error_shape, shaped((64, 512), f32)), low
    )
    parts = gradients(1, mine)
    a_last, copies = pl.pallas_call(
        lambda *refs: last_update_kernel(scale, *refs),
        out_shape=(shaped((64, 256), f32), shaped((4, 16, 512), f32)),
        in_specs=[smem()] + vmem(3),
        compiler_params=VMEM,
    )(idx, parts, a_next, up_next)
    quarters = exchange(copies, Q)
    change, b_last = call(
        change_kernel, (shaped((512, 256), bf16), shaped((64, 512), f32)), a_last, quarters, a_start, up_start
    )
    merged = exchange(change.reshape(16, 32, 256), W)
    new_base = call(merge_kernel, shaped(base.shape[::-1], f32), merged, base.T)
    return (new_base.T, a_last[None], b_last.T[None])


def solution(mesh):
    finer = Mesh(mesh.devices.reshape(4, 2, 2, 2, NZ, 2), (*W, *F))
    return jax.shard_map(
        whole_step,
        mesh=finer,
        in_specs=(
            P(W, None, F, None),
            P(W, None, F, None),
            P(F, W),
            P(W, None, F),
            P(W, None, None),
        ),
        out_specs=(P(F, W), P(W, None, F), P(W, None, None)),
        check_vma=False,
    )
```

```python
import jax
import jax.numpy as jnp
from jax import lax
from jax.experimental import pallas as pl
from jax.experimental.pallas import tpu as pltpu
from jax.sharding import Mesh
from jax.sharding import PartitionSpec as P

W = ("x", "yh", "c")
F = ("yl", "zh", "zl")
Q = ("yl", "zl")
NZ = 8


branch_scale = 0.25
rate_down = 200.0
rate_up = 20.0

bf16 = jnp.bfloat16
f32 = jnp.float32
HIGH = lax.Precision.HIGHEST
VMEM = pltpu.CompilerParams(vmem_limit_bytes=60 * 1024 * 1024)


def dot(a, b, ca, cb, precision=None):
    return lax.dot_general(a, b, (((ca,), (cb,)), ((), ())), precision=precision, preferred_element_type=f32)


def split(value):
    hi = value.astype(bf16)
    return hi, (value - hi.astype(f32)).astype(bf16)


def vmem(n):
    return [pl.BlockSpec(memory_space=pltpu.VMEM)] * n


def smem():
    return pl.BlockSpec(memory_space=pltpu.SMEM)


def start_kernel(base, a_ref, out):
    for z in range(NZ):
        out[z, :32] = base[...].astype(bf16)
        out[z, 32:] = a_ref[...].astype(bf16)


def pack_kernel(idx, x_ref, *outs):
    yl, zl = idx[3], idx[5]
    n = 256
    for k, out in enumerate(outs):
        start = lax.rem(yl + k % 2, 2) * (2 * NZ * n) + lax.rem(zl + k // 2, 2) * n
        for z in range(NZ):
            out[0, :, z * n : (z + 1) * n] = x_ref[0, :, pl.ds(pl.multiple_of(start + z * 2 * n, n), n)]


def wide(value):
    return jnp.concatenate([value[16 * k : 16 * k + 16] for k in range(4)], axis=1)


def tall(value):
    n = value.shape[1] // 4
    return jnp.concatenate([value[:, k * n : k * n + n] for k in range(4)], axis=0)


def group_at(idx, k):
    return 2 * lax.rem(idx[3] + k % 2, 2) + lax.rem(idx[5] + k // 2, 2)


def keys_kernel(step, scale, idx, *rest):
    x_refs, pieces, y_ref, out, bs = rest[:4], rest[4:12], rest[12], rest[-2], rest[-1]
    rows, quarter = x_refs[0].shape[1:]
    px, pyh, pc = idx[0], idx[1], idx[2]
    places = [group_at(idx, k) for k in range(4)]
    tokens = jnp.concatenate([ref[0] for ref in x_refs], axis=0)
    if step == 0:
        whole = rest[13]
        a_half = jnp.concatenate([whole[z, 32:] for z in range(NZ)], axis=1)
        low = dot(a_half, tokens, 1, 1) * scale
        for k in range(4):
            hi, lo = split(low[:, k * rows : (k + 1) * rows])
            out[places[k], rows : rows + 16] = wide(hi)
            out[places[k], rows + 16 :] = wide(lo)
    for dx in range(4):
        for dc in range(2):
            for dy in range(2):
                w = lax.rem(pyh + dy, 2) * 2 + lax.rem(pc + dc, 2)
                bs[dx, w] = pieces[4 * dc + dx][dy]
        at = pl.ds(pl.multiple_of(lax.rem(px + 4 - dx, 4) * 128, 128), 128)
        part = dot(tokens, bs[dx].reshape(128, quarter), 1, 1) * scale
        for k in range(4):
            value = part[k * rows : (k + 1) * rows]
            if k == 0:
                value = value - y_ref[0, :, at].astype(f32)
            out[places[k], :rows, at] = value.astype(bf16)


def low_kernel(scale, idx, keys, whole, *rest):
    x_refs, out, held, sem = rest[:4], rest[4], rest[5], rest[6]
    rows = x_refs[0].shape[1]
    a_half = jnp.concatenate([whole[z, :64] for z in range(NZ)], axis=1)
    low = dot(a_half, jnp.concatenate([ref[0] for ref in x_refs], axis=0), 1, 1) * scale
    quarter = jnp.concatenate([whole[z, 64:] for z in range(NZ)], axis=0)
    for k in range(4):
        at = group_at(idx, k)
        hi, lo = split(low[:, k * rows : (k + 1) * rows])
        held[at, :, :128] = hi
        held[at, :, 128:256] = lo
        held[at, :, 256:] = quarter
    copy = pltpu.make_async_copy(held, out.at[:, rows:, :], sem)
    copy.start()
    copy.wait()


def quarter_of(blocks):
    value = blocks[:, :128].astype(f32) + blocks[:, 128:].astype(f32)
    halves = [
        jnp.concatenate([value[8 * (4 * r + c) : 8 * (4 * r + c) + 8] for c in range(4)], axis=1) for r in range(2)
    ]
    return jnp.concatenate(halves, axis=0)


def error_of(total_rows, keys, low, up, out):
    error = (keys + branch_scale * dot(low, up, 0, 0, HIGH)) / total_rows
    back = wide((branch_scale * dot(up, error, 1, 1, HIGH)).astype(bf16))
    hi, lo = split(branch_scale * dot(low, error, 1, 0, HIGH))
    for q in range(4):
        out[q, :16] = back
        out[q, 16:32] = hi[16 * q : 16 * q + 16]
        out[q, 32:] = lo[16 * q : 16 * q + 16]


def first_error_kernel(total_rows, parts, up_ref, out):
    rows = parts.shape[1] - 32
    k = [parts[q, :rows].astype(f32) for q in range(4)]
    low = [tall(parts[q, rows : rows + 16]).astype(f32) + tall(parts[q, rows + 16 :]).astype(f32) for q in range(4)]
    error_of(total_rows, (k[0] + k[1]) + (k[2] + k[3]), (low[0] + low[1]) + (low[2] + low[3]), up_ref[...], out)


def second_error_kernel(total_rows, parts, out, up_out):
    rows = parts.shape[1] - 64
    k = [parts[q, :rows].astype(f32) for q in range(4)]
    low = [parts[q, rows:, :128].astype(f32) + parts[q, rows:, 128:256].astype(f32) for q in range(4)]
    up = jnp.concatenate([quarter_of(parts[q, rows:, 256:]) for q in range(4)], axis=0)
    up_out[...] = up
    error_of(total_rows, (k[0] + k[1]) + (k[2] + k[3]), (low[0] + low[1]) + (low[2] + low[3]), up, out)


def down_kernel(whole_quarter, idx, parts, *rest):
    x_refs, out = rest[:4], rest[4]
    back = jnp.concatenate([tall(parts[group_at(idx, k), :16]) for k in range(4)], axis=1)
    grads = [parts[q, 16:32].astype(f32) + parts[q, 32:].astype(f32) for q in range(4)]
    hi, lo = split((grads[0] + grads[1]) + (grads[2] + grads[3]))
    tokens = jnp.concatenate([ref[0] for ref in x_refs], axis=0)
    n = out.shape[2]
    for z in range(NZ):
        out[z, :64] = dot(back, tokens[:, z * n : (z + 1) * n], 1, 0).astype(bf16)
        r, c = z // 4, z % 4
        if whole_quarter:
            out[z, 64:80] = hi[:, :n]
            out[z, 80:96] = hi[:, n:]
        else:
            out[z, 64:, :128] = hi[8 * r : 8 * r + 8, 128 * c : 128 * c + 128]
            out[z, 64:, 128:] = lo[8 * r : 8 * r + 8, 128 * c : 128 * c + 128]


def summed(parts):
    result = parts[0].astype(f32)
    for k in range(1, parts.shape[0]):
        result = result + parts[k].astype(f32)
    return result


def update_kernel(scale, parts, a_ref, b_ref, a_out, copies):
    grads = summed(parts)
    a = a_ref[...] - (rate_down * scale) * grads[:64]
    hi, lo = split(b_ref[...] - rate_up * (grads[64:, :128] + grads[64:, 128:]))
    a_out[...] = a
    a_half = a.astype(bf16)
    for z in range(NZ):
        copies[z, :64] = a_half
        copies[z, 64:, :128] = hi
        copies[z, 64:, 128:] = lo


def last_update_kernel(scale, idx, parts, a_ref, up_ref, a_out, copies):
    grads = summed(parts)
    a_out[...] = a_ref[...] - (rate_down * scale) * grads[:64]
    at = pl.ds(pl.multiple_of(16 * group_at(idx, 0), 16), 16)
    b = up_ref[at, :] - rate_up * jnp.concatenate([grads[64:80], grads[80:96]], axis=1)
    for q in range(4):
        copies[q] = b


def change_kernel(a_ref, quarters, a_start, up_start, out, b_out):
    up = jnp.concatenate([quarters[q] for q in range(4)], axis=0)
    left = jnp.concatenate([up, -up_start[...]], axis=0)
    right = jnp.concatenate([a_ref[...], a_start[...]], axis=0)
    out[...] = (branch_scale * dot(left, right, 0, 0, HIGH)).astype(bf16)
    b_out[...] = up


def merge_kernel(parts, base, out):
    out[...] = base[...] + summed(parts) * (1.0 / parts.shape[0])


def shaped(dims, kind):
    return jax.ShapeDtypeStruct(dims, kind)


def call(kernel, shapes, *args):
    return pl.pallas_call(kernel, out_shape=shapes, in_specs=vmem(len(args)), compiler_params=VMEM)(*args)


def pack(idx, tokens):
    steps, rows, width = tokens.shape
    quarter = width // 4
    return pl.pallas_call(
        pack_kernel,
        out_shape=[shaped((steps, rows, quarter), bf16)] * 4,
        grid_spec=pltpu.PrefetchScalarGridSpec(
            num_scalar_prefetch=1,
            grid=(steps,),
            in_specs=[pl.BlockSpec((1, rows, width), lambda i, s: (i, 0, 0))],
            out_specs=[pl.BlockSpec((1, rows, quarter), lambda i, s: (i, 0, 0))] * 4,
        ),
        compiler_params=VMEM,
    )(idx, tokens)


def token_specs(step, xs):
    return [pl.BlockSpec((1, *x.shape[1:]), lambda i, s: (step, 0, 0)) for x in xs]


def with_tokens(kernel, step, shape, idx, args, xs):
    return pl.pallas_call(
        kernel,
        out_shape=shape,
        grid_spec=pltpu.PrefetchScalarGridSpec(
            num_scalar_prefetch=1,
            grid=(1,),
            in_specs=[pl.BlockSpec(a.shape, lambda i, s, n=a.ndim: (0,) * n) for a in args]
            + token_specs(step, xs),
            out_specs=pl.BlockSpec(shape.shape, lambda i, s, n=len(shape.shape): (0,) * n),
        ),
        compiler_params=VMEM,
    )(idx, *args, *xs)


def keys_of(step, scale, idx, shape, xs, targets, pieces, *more):
    _, rows, quarter = xs[0].shape

    def body(*refs):
        keys_kernel(step, scale, *refs)

    return pl.pallas_call(
        body,
        out_shape=shape,
        grid_spec=pltpu.PrefetchScalarGridSpec(
            num_scalar_prefetch=1,
            grid=(1,),
            in_specs=token_specs(step, xs)
            + [pl.BlockSpec(a.shape, lambda i, s: (0, 0, 0)) for a in pieces]
            + [pl.BlockSpec((1, rows, 512), lambda i, s: (step, 0, 0))]
            + [pl.BlockSpec(a.shape, lambda i, s: (0, 0, 0)) for a in more],
            out_specs=pl.BlockSpec((4, rows + 32 * (1 - step), 512), lambda i, s: (0, 0, 0)),
            scratch_shapes=[pltpu.VMEM((4, 4, 32, quarter), bf16)],
        ),
        compiler_params=VMEM,
    )(idx, *xs, *pieces, targets, *more)


def low_of(scale, idx, keys, whole, xs):
    def body(*refs):
        low_kernel(scale, *refs)

    return pl.pallas_call(
        body,
        out_shape=shaped(keys.shape, bf16),
        grid_spec=pltpu.PrefetchScalarGridSpec(
            num_scalar_prefetch=1,
            grid=(1,),
            in_specs=[pl.BlockSpec(memory_space=pl.ANY), pl.BlockSpec(whole.shape, lambda i, s: (0, 0, 0))]
            + token_specs(1, xs),
            out_specs=pl.BlockSpec(memory_space=pl.ANY),
            scratch_shapes=[pltpu.VMEM((4, 64, 512), bf16), pltpu.SemaphoreType.DMA],
        ),
        input_output_aliases={1: 0},
        compiler_params=VMEM,
    )(idx, keys, whole, *xs)


def swap(value, axis):
    return lax.ppermute(value, axis, [(0, 1), (1, 0)])


def swap_both(value):
    return lax.ppermute(value, Q, [(k, 3 - k) for k in range(4)])


def shift(value, axis, by, count):
    return lax.ppermute(value, axis, [(i, (i + by) % count) for i in range(count)])


def exchange(parts, axis):
    return lax.all_to_all(parts, axis, 0, 0, tiled=True)


def whole_step(inputs, targets, base, adapter_a, adapter_b):
    tokens = inputs[0]
    a_start = adapter_a[0]
    _, rows, width = tokens.shape
    scale = width ** (-0.5)
    total_rows = float(rows * 4 * NZ)
    idx = jnp.stack([lax.axis_index(n) for n in (*W, *F[:1], "zh", "zl")]).astype(jnp.int32)
    up_start = adapter_b[0].T
    group = 2 * lax.axis_index("yl") + lax.axis_index("zl")
    z = lax.axis_index("zh")
    block = lax.dynamic_slice(up_start, (16 * group + 8 * (z // 4), 128 * (z % 4)), (8, 128))

    own, to_y, to_z, to_both = pack(idx, tokens)
    xs = (own, swap(to_y, "yl"), swap(to_z, "zl"), swap_both(to_both))
    whole = exchange(call(start_kernel, shaped((NZ, 96, 256), bf16), base.T, a_start), "zh")
    cols = whole[:, :32].transpose(1, 0, 2).reshape(32, width // 4)
    pair = jnp.stack([cols, swap(cols, "yh")])
    near = [pair] + [shift(pair, "x", d, 4) for d in (1, 2, 3)]
    pieces = near + [swap(piece, "c") for piece in near]

    error_shape = shaped((4, 48, 512), bf16)

    def gradients(step, mine):
        shared = exchange(mine, Q)

        def body(*refs):
            down_kernel(step == 1, *refs)

        shape = shaped((NZ, 96 if step else 72, 256), bf16)
        return exchange(with_tokens(body, step, shape, idx, (shared,), xs), "zh")

    keys = keys_of(0, scale, idx, shaped((4, rows + 32, 512), bf16), xs, targets[0], pieces, whole)
    parts = exchange(keys, Q)
    mine = call(lambda *refs: first_error_kernel(total_rows, *refs), error_shape, parts, up_start)
    parts = gradients(0, mine)

    keys = keys_of(1, scale, idx, shaped((4, rows + 64, 512), bf16), xs, targets[0], pieces)
    a_next, copies = call(
        lambda *refs: update_kernel(scale, *refs),
        (shaped((64, 256), f32), shaped((NZ, 72, 256), bf16)),
        parts,
        a_start,
        block,
    )
    whole = exchange(copies, "zh")
    low = exchange(low_of(scale, idx, keys, whole, xs), Q)
    mine, up_next = call(
        lambda *refs: second_error_kernel(total_rows, *refs), (error_shape, shaped((64, 512), f32)), low
    )
    parts = gradients(1, mine)
    a_last, copies = pl.pallas_call(
        lambda *refs: last_update_kernel(scale, *refs),
        out_shape=(shaped((64, 256), f32), shaped((4, 16, 512), f32)),
        in_specs=[smem()] + vmem(3),
        compiler_params=VMEM,
    )(idx, parts, a_next, up_next)
    quarters = exchange(copies, Q)
    change, b_last = call(
        change_kernel, (shaped((512, 256), bf16), shaped((64, 512), f32)), a_last, quarters, a_start, up_start
    )
    merged = exchange(change.reshape(16, 32, 256), W)
    new_base = call(merge_kernel, shaped(base.shape[::-1], f32), merged, base.T)
    return (new_base.T, a_last[None], b_last.T[None])


def solution(mesh):
    finer = Mesh(mesh.devices.reshape(4, 2, 2, 2, NZ, 2), (*W, *F))
    return jax.shard_map(
        whole_step,
        mesh=finer,
        in_specs=(
            P(W, None, F, None),
            P(W, None, F, None),
            P(F, W),
            P(W, None, F),
            P(W, None, None),
        ),
        out_specs=(P(F, W), P(W, None, F), P(W, None, None)),
        check_vma=False,
    )
```

```python
import jax
import jax.numpy as jnp
from jax import lax
from jax.experimental import pallas as pl
from jax.experimental.pallas import tpu as pltpu
from jax.sharding import Mesh
from jax.sharding import PartitionSpec as P

W = ("x", "yh", "c")
F = ("yl", "zh", "zl")
Q = ("yl", "zl")
NZ = 8


branch_scale = 0.25
rate_down = 200.0
rate_up = 20.0

bf16 = jnp.bfloat16
f32 = jnp.float32
VMEM = pltpu.CompilerParams(vmem_limit_bytes=60 * 1024 * 1024)


def dot(a, b, ca, cb):
    return lax.dot_general(a, b, (((ca,), (cb,)), ((), ())), preferred_element_type=f32)


def fine_dot(a, b, ca, cb):
    a_hi, a_lo = split(a)
    b_hi, b_lo = split(b)
    return dot(a_hi, b_hi, ca, cb) + (dot(a_hi, b_lo, ca, cb) + dot(a_lo, b_hi, ca, cb))


def split(value):
    hi = value.astype(bf16)
    return hi, (value - hi.astype(f32)).astype(bf16)


def vmem(n):
    return [pl.BlockSpec(memory_space=pltpu.VMEM)] * n


def smem():
    return pl.BlockSpec(memory_space=pltpu.SMEM)


def start_kernel(base, a_ref, cols, downs):
    for z in range(NZ):
        cols[z] = base[...].astype(bf16)
        downs[z] = a_ref[...].astype(bf16)


def pack_kernel(idx, x_ref, *outs):
    yl, zl = idx[3], idx[5]
    n = 256
    for k, out in enumerate(outs):
        start = lax.rem(yl + k % 2, 2) * (2 * NZ * n) + lax.rem(zl + k // 2, 2) * n
        for z in range(NZ):
            out[0, :, z * n : (z + 1) * n] = x_ref[0, :, pl.ds(pl.multiple_of(start + z * 2 * n, n), n)]


def wide(value):
    return jnp.concatenate([value[16 * k : 16 * k + 16] for k in range(4)], axis=1)


def tall(value):
    n = value.shape[1] // 4
    return jnp.concatenate([value[:, k * n : k * n + n] for k in range(4)], axis=0)


def group_at(idx, k):
    return 2 * lax.rem(idx[3] + k % 2, 2) + lax.rem(idx[5] + k // 2, 2)


def partial_low(whole, tokens):
    return dot(jnp.concatenate([whole[z, :64] for z in range(NZ)], axis=1), tokens, 1, 1)


def keys_kernel(step, scale, idx, *rest):
    x_refs, pieces, y_ref, out, bs = rest[:4], rest[4:12], rest[12], rest[-2], rest[-1]
    rows, quarter = x_refs[0].shape[1:]
    px, pyh, pc = idx[0], idx[1], idx[2]
    places = [group_at(idx, k) for k in range(4)]
    tokens = jnp.concatenate([ref[0] for ref in x_refs], axis=0)
    if step == 0:
        low = partial_low(rest[13], tokens) * scale
        for k in range(4):
            hi, lo = split(low[:, k * rows : (k + 1) * rows])
            out[places[k], rows : rows + 16] = wide(hi)
            out[places[k], rows + 16 :] = wide(lo)
    for dx in range(4):
        for dc in range(2):
            for dy in range(2):
                w = lax.rem(pyh + dy, 2) * 2 + lax.rem(pc + dc, 2)
                bs[dx, w] = pieces[4 * dc + dx][dy]
        at = pl.ds(pl.multiple_of(lax.rem(px + 4 - dx, 4) * 128, 128), 128)
        part = dot(tokens, bs[dx].reshape(128, quarter), 1, 1) * scale
        for k in range(4):
            value = part[k * rows : (k + 1) * rows]
            if k == 0:
                value = value - y_ref[0, :, at].astype(f32)
            out[places[k], :rows, at] = value.astype(bf16)


def low_kernel(scale, idx, keys, whole, *rest):
    x_refs, out, held, sem = rest[:4], rest[4], rest[5], rest[6]
    rows = x_refs[0].shape[1]
    low = partial_low(whole, jnp.concatenate([ref[0] for ref in x_refs], axis=0)) * scale
    quarter = jnp.concatenate([whole[z, 64:] for z in range(NZ)], axis=0)
    for k in range(4):
        at = group_at(idx, k)
        hi, lo = split(low[:, k * rows : (k + 1) * rows])
        held[at, :, :128] = hi
        held[at, :, 128:256] = lo
        held[at, :, 256:] = quarter
    copy = pltpu.make_async_copy(held, out.at[:, rows:, :], sem)
    copy.start()
    copy.wait()


def quarter_of(blocks):
    value = blocks[:, :128].astype(f32) + blocks[:, 128:].astype(f32)
    halves = [
        jnp.concatenate([value[8 * (4 * r + c) : 8 * (4 * r + c) + 8] for c in range(4)], axis=1) for r in range(2)
    ]
    return jnp.concatenate(halves, axis=0)


def error_of(total_rows, keys, low, up, out):
    error = (keys + branch_scale * fine_dot(low, up, 0, 0)) / total_rows
    back = wide((branch_scale * fine_dot(up, error, 1, 1)).astype(bf16))
    hi, lo = split(branch_scale * fine_dot(low, error, 1, 0))
    for q in range(4):
        out[q, :16] = back
        out[q, 16:32] = hi[16 * q : 16 * q + 16]
        out[q, 32:] = lo[16 * q : 16 * q + 16]


def first_error_kernel(total_rows, parts, up_ref, out):
    rows = parts.shape[1] - 32
    k = [parts[q, :rows].astype(f32) for q in range(4)]
    low = [tall(parts[q, rows : rows + 16]).astype(f32) + tall(parts[q, rows + 16 :]).astype(f32) for q in range(4)]
    error_of(total_rows, (k[0] + k[1]) + (k[2] + k[3]), (low[0] + low[1]) + (low[2] + low[3]), up_ref[...], out)


def second_error_kernel(total_rows, parts, out, up_out):
    rows = parts.shape[1] - 64
    k = [parts[q, :rows].astype(f32) for q in range(4)]
    low = [parts[q, rows:, :128].astype(f32) + parts[q, rows:, 128:256].astype(f32) for q in range(4)]
    up = jnp.concatenate([quarter_of(parts[q, rows:, 256:]) for q in range(4)], axis=0)
    up_out[...] = up
    error_of(total_rows, (k[0] + k[1]) + (k[2] + k[3]), (low[0] + low[1]) + (low[2] + low[3]), up, out)


def down_kernel(whole_quarter, idx, parts, *rest):
    x_refs, out = rest[:4], rest[4]
    back = jnp.concatenate([tall(parts[group_at(idx, k), :16]) for k in range(4)], axis=1)
    grads = [parts[q, 16:32].astype(f32) + parts[q, 32:].astype(f32) for q in range(4)]
    hi, lo = split((grads[0] + grads[1]) + (grads[2] + grads[3]))
    tokens = jnp.concatenate([ref[0] for ref in x_refs], axis=0)
    n = out.shape[2]
    for z in range(NZ):
        out[z, :64] = dot(back, tokens[:, z * n : (z + 1) * n], 1, 0).astype(bf16)
        r, c = z // 4, z % 4
        if whole_quarter:
            out[z, 64:80] = hi[:, :n]
            out[z, 80:96] = hi[:, n:]
        else:
            out[z, 64:, :128] = hi[8 * r : 8 * r + 8, 128 * c : 128 * c + 128]
            out[z, 64:, 128:] = lo[8 * r : 8 * r + 8, 128 * c : 128 * c + 128]


def summed(parts):
    result = parts[0].astype(f32)
    for k in range(1, parts.shape[0]):
        result = result + parts[k].astype(f32)
    return result


def update_kernel(scale, parts, a_ref, b_ref, a_out, copies):
    grads = summed(parts)
    a = a_ref[...] - (rate_down * scale) * grads[:64]
    hi, lo = split(b_ref[...] - rate_up * (grads[64:, :128] + grads[64:, 128:]))
    a_out[...] = a
    a_half = a.astype(bf16)
    for z in range(NZ):
        copies[z, :64] = a_half
        copies[z, 64:, :128] = hi
        copies[z, 64:, 128:] = lo


def last_update_kernel(scale, idx, parts, a_ref, up_ref, a_out, copies):
    grads = summed(parts)
    a_out[...] = a_ref[...] - (rate_down * scale) * grads[:64]
    at = pl.ds(pl.multiple_of(16 * group_at(idx, 0), 16), 16)
    b = up_ref[at, :] - rate_up * jnp.concatenate([grads[64:80], grads[80:96]], axis=1)
    for q in range(4):
        copies[q] = b


def change_kernel(a_ref, quarters, a_start, up_start, out, b_out):
    up = jnp.concatenate([quarters[q] for q in range(4)], axis=0)
    left = jnp.concatenate([up, -up_start[...]], axis=0)
    right = jnp.concatenate([a_ref[...], a_start[...]], axis=0)
    out[...] = (branch_scale * fine_dot(left, right, 0, 0)).astype(bf16)
    b_out[...] = up


def merge_kernel(parts, base, out):
    out[...] = base[...] + summed(parts) * (1.0 / parts.shape[0])


def shaped(dims, kind):
    return jax.ShapeDtypeStruct(dims, kind)


def call(kernel, shapes, *args):
    return pl.pallas_call(kernel, out_shape=shapes, in_specs=vmem(len(args)), compiler_params=VMEM)(*args)


def pack(idx, tokens):
    steps, rows, width = tokens.shape
    quarter = width // 4
    return pl.pallas_call(
        pack_kernel,
        out_shape=[shaped((steps, rows, quarter), bf16)] * 4,
        grid_spec=pltpu.PrefetchScalarGridSpec(
            num_scalar_prefetch=1,
            grid=(steps,),
            in_specs=[pl.BlockSpec((1, rows, width), lambda i, s: (i, 0, 0))],
            out_specs=[pl.BlockSpec((1, rows, quarter), lambda i, s: (i, 0, 0))] * 4,
        ),
        compiler_params=VMEM,
    )(idx, tokens)


def with_tokens(kernel, step, shape, idx, args, xs):
    _, rows, quarter = xs[0].shape
    return pl.pallas_call(
        kernel,
        out_shape=shape,
        grid_spec=pltpu.PrefetchScalarGridSpec(
            num_scalar_prefetch=1,
            grid=(1,),
            in_specs=[pl.BlockSpec(a.shape, lambda i, s, n=a.ndim: (0,) * n) for a in args]
            + [pl.BlockSpec((1, rows, quarter), lambda i, s: (step, 0, 0))] * 4,
            out_specs=pl.BlockSpec(shape.shape, lambda i, s, n=len(shape.shape): (0,) * n),
        ),
        compiler_params=VMEM,
    )(idx, *args, *xs)


def keys_of(step, scale, idx, shape, xs, targets, pieces, *more):
    _, rows, quarter = xs[0].shape

    def body(*refs):
        keys_kernel(step, scale, *refs)

    return pl.pallas_call(
        body,
        out_shape=shape,
        grid_spec=pltpu.PrefetchScalarGridSpec(
            num_scalar_prefetch=1,
            grid=(1,),
            in_specs=[pl.BlockSpec((1, rows, quarter), lambda i, s: (step, 0, 0))] * 4
            + [pl.BlockSpec(a.shape, lambda i, s: (0, 0, 0)) for a in pieces]
            + [pl.BlockSpec((1, rows, 512), lambda i, s: (step, 0, 0))]
            + [pl.BlockSpec(a.shape, lambda i, s: (0, 0, 0)) for a in more],
            out_specs=pl.BlockSpec((4, rows + 32 * (1 - step), 512), lambda i, s: (0, 0, 0)),
            scratch_shapes=[pltpu.VMEM((4, 4, 32, quarter), bf16)],
        ),
        compiler_params=VMEM,
    )(idx, *xs, *pieces, targets, *more)


def low_of(scale, idx, keys, whole, xs):
    _, rows, quarter = xs[0].shape

    def body(*refs):
        low_kernel(scale, *refs)

    return pl.pallas_call(
        body,
        out_shape=shaped(keys.shape, bf16),
        grid_spec=pltpu.PrefetchScalarGridSpec(
            num_scalar_prefetch=1,
            grid=(1,),
            in_specs=[pl.BlockSpec(memory_space=pl.ANY), pl.BlockSpec(whole.shape, lambda i, s: (0, 0, 0))]
            + [pl.BlockSpec((1, rows, quarter), lambda i, s: (1, 0, 0))] * 4,
            out_specs=pl.BlockSpec(memory_space=pl.ANY),
            scratch_shapes=[pltpu.VMEM((4, 64, 512), bf16), pltpu.SemaphoreType.DMA],
        ),
        input_output_aliases={1: 0},
        compiler_params=VMEM,
    )(idx, keys, whole, *xs)


def swap(value, axis):
    return lax.ppermute(value, axis, [(0, 1), (1, 0)])


def swap_both(value):
    return lax.ppermute(value, Q, [(k, 3 - k) for k in range(4)])


def shift(value, axis, by, count):
    return lax.ppermute(value, axis, [(i, (i + by) % count) for i in range(count)])


def exchange(parts, axis):
    return lax.all_to_all(parts, axis, 0, 0, tiled=True)


def whole_step(inputs, targets, base, adapter_a, adapter_b):
    tokens = inputs[0]
    a_start = adapter_a[0]
    _, rows, width = tokens.shape
    scale = width ** (-0.5)
    total_rows = float(rows * 4 * NZ)
    idx = jnp.stack([lax.axis_index(n) for n in (*W, *F[:1], "zh", "zl")]).astype(jnp.int32)
    up_start = adapter_b[0].T
    group = 2 * lax.axis_index("yl") + lax.axis_index("zl")
    z = lax.axis_index("zh")
    block = lax.dynamic_slice(up_start, (16 * group + 8 * (z // 4), 128 * (z % 4)), (8, 128))

    own, to_y, to_z, to_both = pack(idx, tokens)
    xs = (own, swap(to_y, "yl"), swap(to_z, "zl"), swap_both(to_both))
    columns, downs = call(
        start_kernel, (shaped((NZ, 32, 256), bf16), shaped((NZ, 64, 256), bf16)), base.T, a_start
    )
    cols = exchange(columns, "zh")
    cols = cols.transpose(1, 0, 2).reshape(cols.shape[1], width // 4)
    pair = jnp.stack([cols, swap(cols, "yh")])
    near = [pair] + [shift(pair, "x", d, 4) for d in (1, 2, 3)]
    whole = exchange(downs, "zh")
    pieces = near + [swap(piece, "c") for piece in near]

    error_shape = shaped((4, 48, 512), bf16)

    def gradients(step, mine):
        shared = exchange(mine, Q)

        def body(*refs):
            down_kernel(step == 1, *refs)

        shape = shaped((NZ, 96 if step else 72, 256), bf16)
        return exchange(with_tokens(body, step, shape, idx, (shared,), xs), "zh")

    keys = keys_of(0, scale, idx, shaped((4, rows + 32, 512), bf16), xs, targets[0], pieces, whole)
    parts = exchange(keys, Q)
    mine = call(lambda *refs: first_error_kernel(total_rows, *refs), error_shape, parts, up_start)
    parts = gradients(0, mine)

    keys = keys_of(1, scale, idx, shaped((4, rows + 64, 512), bf16), xs, targets[0], pieces)
    a_next, copies = call(
        lambda *refs: update_kernel(scale, *refs),
        (shaped((64, 256), f32), shaped((NZ, 72, 256), bf16)),
        parts,
        a_start,
        block,
    )
    whole = exchange(copies, "zh")
    low = exchange(low_of(scale, idx, keys, whole, xs), Q)
    mine, up_next = call(
        lambda *refs: second_error_kernel(total_rows, *refs), (error_shape, shaped((64, 512), f32)), low
    )
    parts = gradients(1, mine)
    a_last, copies = pl.pallas_call(
        lambda *refs: last_update_kernel(scale, *refs),
        out_shape=(shaped((64, 256), f32), shaped((4, 16, 512), f32)),
        in_specs=[smem()] + vmem(3),
        compiler_params=VMEM,
    )(idx, parts, a_next, up_next)
    quarters = exchange(copies, Q)
    change, b_last = call(
        change_kernel, (shaped((512, 256), bf16), shaped((64, 512), f32)), a_last, quarters, a_start, up_start
    )
    merged = exchange(change.reshape(16, 32, 256), W)
    new_base = call(merge_kernel, shaped(base.shape[::-1], f32), merged, base.T)
    return (new_base.T, a_last[None], b_last.T[None])


def solution(mesh):
    finer = Mesh(mesh.devices.reshape(4, 2, 2, 2, NZ, 2), (*W, *F))
    return jax.shard_map(
        whole_step,
        mesh=finer,
        in_specs=(
            P(W, None, F, None),
            P(W, None, F, None),
            P(F, W),
            P(W, None, F),
            P(W, None, None),
        ),
        out_specs=(P(F, W), P(W, None, F), P(W, None, None)),
        check_vma=False,
    )
```
